32 devices in a mesh: groups: 2 (over x), streams: 16 (over z, y, core).
Axes of the slice: x: 2, y: 2, z: 4, core: 2. Of those that a mesh axis runs over, the one named last changes fastest.
Arguments:
- frames: bfloat16 [4096, 1536], P(('groups', 'streams')), parts along dimension 0, may hold values from -500 to 500
- route_peer: int32 [4096], P(('groups', 'streams')), parts along dimension 0, may hold values from 0 to 15, as said below
- route_pos: int32 [4096], P(('groups', 'streams')), parts along dimension 0, may hold values from 0 to 127
- destination: int32 [256], P(('groups', 'streams')), parts along dimension 0, may hold values from 0 to 127, as said below
- valid_count: int32 [256], P(('groups', 'streams')), parts along dimension 0, may hold values from 1 to 16
- key_cache: bfloat16 [256, 32, 768], P(('groups', 'streams')), parts along dimension 0, may hold values from -700 to 700
- value_cache: bfloat16 [256, 32, 768], P(('groups', 'streams')), parts along dimension 0, may hold values from -4 to 4
- conv_state: bfloat16 [256, 31, 768], P(('groups', 'streams')), parts along dimension 0, may hold values from -4 to 4
- qkv_weight: bfloat16 [1536, 2304], replicated, may hold values from -0.15625 to 0.15625
- conv_kernel: bfloat16 [32, 768], replicated, may hold values from -1 to 1
Outputs:
- encoded: bfloat16 [4096, 768], P(('groups', 'streams')), parts along dimension 0
- keys_next: bfloat16 [256, 32, 768], P(('groups', 'streams')), parts along dimension 0
- values_next: bfloat16 [256, 32, 768], P(('groups', 'streams')), parts along dimension 0
- conv_next: bfloat16 [256, 31, 768], P(('groups', 'streams')), parts along dimension 0
The draws below stay inside these ranges and needn't reach their ends.
There are 2 independent parts, one for each index of `groups`. The reference program is written for one: setup_inputs(seed, part) draws one part's arguments, and reference() takes and returns one part's arrays. A program takes and returns all parts, laid end to end along the dimension named above; an argument that names none is the same for every part. Nothing has to cross between parts.
Inputs may be any that keep to these rules, and one draw needn't show every extreme that they name: `route_peer`: each owner slot of a part receives exactly one frame row; the rows one ingest device sends to one owner number at most 12, and exactly 12 to some owner in every draw. `destination`: A permutation of the 128 slots. A stream stays on its device or moves to the device one index up or down along streams, wrapping; at most 4 streams go from one device to each neighbour, and exactly 4 from some device in every draw.
All inputs are finite; a program needn't handle non-finite values.
Results may differ from the reference program's by a relative error of at most 0.0059.
Values may be sent and summed in bfloat16 or wider, within the bound.
No kernel may reach another device: no remote copies, remote signals or barrier semaphores. Data moves between devices by JAX's collectives and lax.ppermute only.
A program may use at most 64 MiB of HBM per device.

```python
import math
import jax
import jax.numpy as jnp
from jax import lax

D = 1536
HEAD = 96
SPAN = 16
LEFT = 32
KERNEL = 32
MIG = 4
S_DEV = 8
HD = 768
ROWS_DEV = 128
STREAMS = 128
FRAMES = 2048


def shuffle_rows(base_key, row_count, length):

    def one_shuffle(single_key):
        return jax.random.permutation(single_key, length).astype(jnp.int32)
    return jax.vmap(one_shuffle)(jax.random.split(base_key, row_count))


def routing(key):
    peer_count = FRAMES // ROWS_DEV
    per_peer = ROWS_DEV // peer_count
    extra = per_peer // 2
    key_offset, key_send, key_recv = jax.random.split(key, 3)
    offsets = jax.random.permutation(key_offset, peer_count - 1).astype(jnp.int32)[:2] + 1
    sender = jnp.arange(peer_count, dtype=jnp.int32)[:, None]
    owner_ids = jnp.arange(peer_count, dtype=jnp.int32)[None, :]
    distance = (owner_ids - sender) % peer_count
    counts = per_peer + extra * (distance == offsets[0]).astype(jnp.int32) - extra * (distance == offsets[1]).astype(jnp.int32)
    block_end = jnp.cumsum(counts, axis=1)
    block_start = block_end - counts
    row_ids = jnp.arange(ROWS_DEV, dtype=jnp.int32)
    peer_of = jnp.sum((block_end[:, None, :] <= row_ids[None, :, None]).astype(jnp.int32), axis=2)
    slot_of = row_ids[None, :] - jnp.take_along_axis(block_start, peer_of, axis=1)
    inbound = jnp.cumsum(counts, axis=0) - counts
    arrival = jnp.take_along_axis(inbound, peer_of, axis=1) + slot_of
    recv_perm = shuffle_rows(key_recv, peer_count, ROWS_DEV)
    position = recv_perm[peer_of, arrival]
    send_perm = shuffle_rows(key_send, peer_count, ROWS_DEV)
    sender_rows = jnp.broadcast_to(sender, (peer_count, ROWS_DEV))
    peer_out = jnp.zeros((peer_count, ROWS_DEV), jnp.int32).at[sender_rows, send_perm].set(peer_of)
    pos_out = jnp.zeros((peer_count, ROWS_DEV), jnp.int32).at[sender_rows, send_perm].set(position)
    return (peer_out.reshape(-1), pos_out.reshape(-1))


def draw_route_peer(key, part):
    return routing(jax.random.fold_in(key, 101))[0]


def draw_route_pos(key, part):
    return routing(jax.random.fold_in(key, 101))[1]


def draw_destination(key, part):
    peer_count = STREAMS // S_DEV
    key_count, key_perm = jax.random.split(jax.random.fold_in(key, 202))
    moving = jax.random.randint(key_count, (peer_count,), 0, MIG + 1).astype(jnp.int32).at[0].set(MIG)
    shuffles = shuffle_rows(key_perm, peer_count, S_DEV)
    device_ids = jnp.arange(peer_count, dtype=jnp.int32)[:, None]
    slot_ids = jnp.arange(S_DEV, dtype=jnp.int32)[None, :]
    going_up = moving[:, None]
    going_down = jnp.roll(moving, 1)[:, None]
    earlier = jnp.roll(moving, 2)[:, None]
    to_upper = slot_ids < going_up
    to_lower = (slot_ids >= going_up) & (slot_ids < going_up + going_down)
    upper_slot = jnp.roll(shuffles, -1, axis=0)
    lower_index = jnp.clip(earlier + slot_ids - going_up, 0, S_DEV - 1)
    lower_slot = jnp.take_along_axis(jnp.roll(shuffles, 1, axis=0), lower_index, axis=1)
    new_device = jnp.where(to_upper, (device_ids + 1) % peer_count, jnp.where(to_lower, (device_ids + peer_count - 1) % peer_count, device_ids))
    new_slot = jnp.where(to_upper, upper_slot, jnp.where(to_lower, lower_slot, shuffles))
    target = new_device * S_DEV + new_slot
    device_rows = jnp.broadcast_to(device_ids, (peer_count, S_DEV))
    result = jnp.zeros((peer_count, S_DEV), jnp.int32).at[device_rows, shuffles].set(target)
    return result.reshape(-1)


def draw_frames(key, part):
    key_a, key_b, key_c = jax.random.split(jax.random.fold_in(key, 303), 3)
    row_scale = jnp.exp(jax.random.uniform(key_a, (FRAMES, 1)) * math.log(10.0))
    col_scale = jnp.exp(jax.random.uniform(key_b, (1, D)) * math.log(10.0))
    base = jnp.clip(jax.random.normal(key_c, (FRAMES, D)), -4.0, 4.0)
    return (base * row_scale * col_scale).astype(jnp.bfloat16)


def draw_key_cache(key, part):
    key_a = jax.random.fold_in(jax.random.fold_in(key, 404), 0)
    return jnp.clip(jax.random.normal(key_a, (STREAMS, LEFT, HD)), -4.0, 4.0).astype(jnp.bfloat16)


def place_ends(entries, stream_key, low, high):
    index_at = [jax.random.randint(jax.random.fold_in(stream_key, axis), (), 0, length) for axis, length in enumerate(entries.shape)]
    main_axis = entries.shape.index(max(entries.shape))
    neighbour = index_at[:main_axis] + [(index_at[main_axis] + 1) % entries.shape[main_axis]] + index_at[main_axis + 1:]
    return entries.at[tuple(index_at)].set(low).at[tuple(neighbour)].set(high)


def shard_levels(stream_key, dims, shards, low, high):
    gain, own = 1.0, jax.random.fold_in(stream_key, 6)
    for axis_at, shards_of in shards:
        draws = jnp.exp(jax.random.uniform(jax.random.fold_in(own, axis_at), (shards_of,), jnp.float32, low / len(shards), high / len(shards)))
        gain = gain * jnp.repeat(draws, dims[axis_at] // shards_of).reshape([-1 if axis == axis_at else 1 for axis in range(len(dims))])
    return gain


def normal_values(rng, shape, deviation, most, cuts=(), kind=jnp.bfloat16):
    loudness = shard_levels(rng, shape, cuts, -0.22, 0.18) if cuts else 1.0
    entries = jax.random.normal(rng, shape, jnp.float32) * deviation * loudness
    return jnp.minimum(jnp.maximum(entries, -most), most).astype(kind)


def setup_inputs(seed: int = 0, part: int = 0) -> dict:
    keys = jax.random.split(jax.random.key(seed), 11)
    own_keys = jax.random.split(jax.random.fold_in(keys[10], part), 11)
    frames = draw_frames(jax.random.fold_in(jax.random.fold_in(keys[10], part), 71), part)
    route_peer = draw_route_peer(jax.random.fold_in(jax.random.fold_in(keys[10], part), 71), part)
    route_pos = draw_route_pos(jax.random.fold_in(jax.random.fold_in(keys[10], part), 71), part)
    destination = draw_destination(jax.random.fold_in(jax.random.fold_in(keys[10], part), 71), part)
    valid_count = place_ends(jax.random.randint(own_keys[4], (STREAMS,), 1, SPAN + 1), jax.random.fold_in(own_keys[4], 1), 1, SPAN).astype(jnp.int32)
    key_cache = draw_key_cache(jax.random.fold_in(jax.random.fold_in(keys[10], part), 71), part)
    value_cache = normal_values(own_keys[6], (STREAMS, LEFT, HD), 1.0, 4.0, ((0, 16),))
    conv_state = normal_values(own_keys[7], (STREAMS, KERNEL - 1, HD), 1.0, 4.0, ((0, 16),))
    qkv_weight = normal_values(keys[8], (D, 3 * HD), D ** -0.5, 0.15625)
    conv_kernel = normal_values(keys[9], (KERNEL, HD), KERNEL ** -0.5, 1.0)
    return dict(frames=frames, route_peer=route_peer, route_pos=route_pos, destination=destination, valid_count=valid_count, key_cache=key_cache, value_cache=value_cache, conv_state=conv_state, qkv_weight=qkv_weight, conv_kernel=conv_kernel)


EPSILON = 1e-05

def layer_norm(matrix):
    widened = matrix.astype(jnp.float32)
    centered = widened - lax.optimization_barrier(jnp.mean(widened, axis=-1, keepdims=True))
    spread = lax.optimization_barrier(jnp.mean(centered * centered, axis=-1, keepdims=True))
    return (centered * lax.rsqrt(spread + EPSILON)).astype(jnp.bfloat16)

def stream_step(qkv_rows, old_keys, old_values, old_conv, valid_count, conv_kernel):
    streams_here, span_len, triple = qkv_rows.shape
    qkv_width = triple // 3
    head_count = qkv_width // HEAD
    left_len = old_keys.shape[1]
    key_len = left_len + span_len
    keys_all = jnp.concatenate([old_keys, qkv_rows[:, :, qkv_width:2 * qkv_width]], axis=1)
    values_all = jnp.concatenate([old_values, qkv_rows[:, :, 2 * qkv_width:]], axis=1)
    query_heads = qkv_rows[:, :, :qkv_width].reshape(streams_here, span_len, head_count, HEAD).astype(jnp.float32)
    key_heads = keys_all.reshape(streams_here, key_len, head_count, HEAD).astype(jnp.float32)
    value_heads = values_all.reshape(streams_here, key_len, head_count, HEAD).astype(jnp.float32)
    scores = jnp.einsum('sqhd,skhd->shqk', query_heads, key_heads) * HEAD ** (-0.5)
    query_pos = jnp.arange(span_len, dtype=jnp.int32)[:, None]
    key_pos = jnp.arange(key_len, dtype=jnp.int32)[None, :] - left_len
    causal = (key_pos <= query_pos)[None]
    filled = key_pos[None] < valid_count[:, None, None]
    allowed = (key_pos[None] < 0) | causal & filled
    scores = jnp.where(allowed[:, None], scores, -1e+30)
    row_max = lax.optimization_barrier(jnp.max(scores, axis=-1, keepdims=True))
    weights_exp = jnp.exp(scores - row_max)
    probabilities = (weights_exp / lax.optimization_barrier(jnp.sum(weights_exp, axis=-1, keepdims=True))).astype(jnp.bfloat16)
    probabilities = lax.optimization_barrier(probabilities)
    mixed_heads = jnp.einsum('shqk,skhd->sqhd', probabilities.astype(jnp.float32), value_heads)
    alive_rows = jnp.arange(span_len, dtype=jnp.int32)[None, :] < valid_count[:, None]
    attended = jnp.where(alive_rows[:, :, None, None], mixed_heads, 0.0)
    attended = attended.reshape(streams_here, span_len, qkv_width).astype(jnp.bfloat16)
    attended = lax.optimization_barrier(attended)
    conv_input = jnp.concatenate([old_conv, attended], axis=1)
    kernel_len = conv_kernel.shape[0]
    summed = attended.astype(jnp.float32)
    for offset_tap in range(kernel_len):
        window = conv_input[:, offset_tap:offset_tap + span_len].astype(jnp.float32)
        summed = summed + conv_kernel[offset_tap].astype(jnp.float32) * window
    encoded = jnp.where(alive_rows[:, :, None], summed, 0.0).astype(jnp.bfloat16)
    key_pick = valid_count[:, None] + jnp.arange(left_len, dtype=jnp.int32)[None, :]
    key_pick = jnp.broadcast_to(key_pick[:, :, None], (streams_here, left_len, qkv_width))
    keys_next = jnp.take_along_axis(keys_all, key_pick, axis=1)
    values_next = jnp.take_along_axis(values_all, key_pick, axis=1)
    conv_pick = valid_count[:, None] + jnp.arange(kernel_len - 1, dtype=jnp.int32)[None, :]
    conv_pick = jnp.broadcast_to(conv_pick[:, :, None], (streams_here, kernel_len - 1, qkv_width))
    conv_next = jnp.take_along_axis(conv_input, conv_pick, axis=1)
    return (encoded.reshape(streams_here * span_len, qkv_width), keys_next, values_next, conv_next)

def reference(frames, route_peer, route_pos, destination, valid_count, key_cache, value_cache, conv_state, qkv_weight, conv_kernel):
    target = route_peer * ROWS_DEV + route_pos
    owned = jnp.zeros_like(frames).at[target].set(frames)
    normed = layer_norm(owned)
    qkv_rows = jnp.dot(normed, qkv_weight, preferred_element_type=jnp.float32).astype(jnp.bfloat16)
    qkv_rows = lax.optimization_barrier(qkv_rows)
    moved_keys = jnp.zeros_like(key_cache).at[destination].set(key_cache)
    moved_values = jnp.zeros_like(value_cache).at[destination].set(value_cache)
    moved_conv = jnp.zeros_like(conv_state).at[destination].set(conv_state)
    encoded, keys_next, values_next, conv_next = stream_step(qkv_rows.reshape(STREAMS, SPAN, 3 * HD), moved_keys, moved_values, moved_conv, valid_count, conv_kernel)
    return (encoded, keys_next, values_next, conv_next)
```

```python
import jax
import jax.numpy as jnp
from jax import lax
from jax.experimental import pallas as pl
from jax.experimental.pallas import tpu as pltpu
from jax.sharding import PartitionSpec as P

HEAD = 96
MIG = 4
EPSILON = 1e-05
LANES = 128
TILE = 8
FOLD = 2

BF16 = jnp.bfloat16
F32 = jnp.float32
I32 = jnp.int32


def iota(shape, axis):
    return lax.broadcasted_iota(I32, shape, axis)


def ones_where(condition):
    return jnp.where(condition, 1.0, 0.0).astype(BF16)


def matmul(left, right):
    return jnp.dot(left, right, preferred_element_type=F32)


def matmul_nt(left, right):
    return lax.dot_general(left, right, (((1,), (1,)), ((), ())), preferred_element_type=F32)


def round_up(value, multiple):
    return -(-value // multiple) * multiple


def whole(*spaces):
    return [pl.BlockSpec(memory_space=space) for space in spaces]


def block_sizes(width, capacity):
    slots = round_up(capacity, TILE // FOLD)
    group_rows = FOLD * slots
    groups = width // FOLD // LANES
    return slots, group_rows, groups, groups * group_rows + TILE


def pack_frames(frames, route_peer, route_pos, peers, capacity):
    row_count, width = frames.shape
    slots, group_rows, groups, block_rows = block_sizes(width, capacity)
    half = width // FOLD

    def body(frames_ref, peer_ref, pos_ref, out_ref):
        peer = peer_ref[...]
        owner = ones_where(iota((peers, row_count), 0) == peer)
        earlier = ones_where(iota((row_count, row_count), 0) < iota((row_count, row_count), 1))
        running = matmul(owner, earlier)
        slot = jnp.sum(running * owner.astype(F32), axis=0, keepdims=True).astype(I32)
        flat = peer * group_rows + slot
        rows = iota((peers * group_rows, row_count), 0)
        pick = jnp.concatenate([ones_where(rows == flat + h * slots) for h in range(FOLD)], axis=1)
        source = jnp.concatenate(
            [frames_ref[:, h * half : (h + 1) * half] for h in range(FOLD)], axis=0
        )
        packed = matmul(pick, source).astype(BF16)
        owner_tile = ones_where(iota((peers * TILE, row_count), 0) // TILE == peer)
        lane = iota((LANES, row_count), 0)
        in_lane = (lane % slots == slot) & (lane < group_rows)
        code = jnp.where(in_lane, (pos_ref[...] + 1).astype(F32), 0.0).astype(BF16)
        codes = matmul_nt(owner_tile, code).astype(BF16)
        for p in range(peers):
            for g in range(groups):
                out_ref[p * block_rows + g * group_rows : p * block_rows + (g + 1) * group_rows, :] = (
                    packed[p * group_rows : (p + 1) * group_rows, g * LANES : (g + 1) * LANES]
                )
            out_ref[(p + 1) * block_rows - TILE : (p + 1) * block_rows, :] = codes[
                p * TILE : (p + 1) * TILE, :
            ]

    return pl.pallas_call(
        body,
        out_shape=jax.ShapeDtypeStruct((peers * block_rows, LANES), BF16),
        in_specs=whole(pltpu.VMEM, pltpu.VMEM, pltpu.VMEM),
        out_specs=pl.BlockSpec(memory_space=pltpu.VMEM),
        name="pack_frames",
    )(frames, route_peer.reshape(1, -1), route_pos.reshape(1, -1))


def pack_streams(destination, key_cache, value_cache, conv_state, peers):
    streams, left, width = key_cache.shape
    tail = conv_state.shape[1]
    rows = 2 * left + 1 + tail

    def body(dest_ref, own_ref, key_ref, value_ref, conv_ref, up_ref, down_ref):
        own = own_ref[0]
        up_ref[...] = jnp.zeros_like(up_ref)
        down_ref[...] = jnp.zeros_like(down_ref)

        def put(out_ref, rank, j, slot):
            out_ref[rank, 0:left, :] = key_ref[j]
            out_ref[rank, left : 2 * left, :] = value_ref[j]
            code = jnp.full((1, width), slot + 1, I32).astype(F32).astype(BF16)
            out_ref[rank, 2 * left : rows, :] = jnp.concatenate([code, conv_ref[j]], axis=0)

        def step(chosen_device, out_ref):
            rank = jnp.int32(0)
            for j in range(streams):
                target = dest_ref[j]
                chosen = target // streams == chosen_device

                @pl.when(chosen)
                def _():
                    put(out_ref, jnp.minimum(rank, MIG - 1), j, target % streams)

                rank = rank + chosen.astype(I32)

        step((own + 1) % peers, up_ref)
        step((own + peers - 1) % peers, down_ref)

    bundle = jax.ShapeDtypeStruct((MIG, rows, width), BF16)
    return pl.pallas_call(
        body,
        out_shape=(bundle, bundle),
        in_specs=whole(pltpu.SMEM, pltpu.SMEM, pltpu.VMEM, pltpu.VMEM, pltpu.VMEM),
        out_specs=whole(pltpu.VMEM, pltpu.VMEM),
        name="pack_streams",
    )(destination, own_index(), key_cache, value_cache, conv_state)


def own_index():
    return lax.axis_index("streams").astype(I32).reshape(1)


def stream_step(
    received, from_lower, from_upper, destination, valid_count, key_cache, value_cache, conv_state,
    qkv_weight, conv_kernel, peers, row_count, capacity,
):
    streams, left, width = key_cache.shape
    tail = conv_state.shape[1]
    taps = conv_kernel.shape[0]
    span = row_count // streams
    model = qkv_weight.shape[0]
    half = model // FOLD
    heads = width // HEAD
    keys = left + span
    window = 1 + tail + span
    slots, group_rows, groups, block_rows = block_sizes(model, capacity)
    packed_rows = peers * group_rows

    def body(
        dest_ref, own_ref, valid_ref, recv_ref, lower_ref, upper_ref, key_ref, value_ref, conv_ref,
        weight_ref, taps_ref, encoded_ref, keys_next_ref, values_next_ref, conv_next_ref,
        gathered, keys_all, values_all, conv_in, taps_f32, encoded_f32,
    ):
        own = own_ref[0]
        for j in range(streams):
            target = dest_ref[j]

            @pl.when(target // streams == own)
            def _():
                slot = target % streams
                keys_all[slot, 0:left, :] = key_ref[j]
                values_all[slot, 0:left, :] = value_ref[j]
                conv_in[slot, 1 : 1 + tail, :] = conv_ref[j].astype(F32)

        for bundle_ref in (lower_ref, upper_ref):
            for j in range(MIG):
                code = jnp.max(bundle_ref[j, 2 * left : 2 * left + 1, :].astype(F32)).astype(I32)

                @pl.when(code > 0)
                def _():
                    keys_all[code - 1, 0:left, :] = bundle_ref[j, 0:left, :]
                    values_all[code - 1, 0:left, :] = bundle_ref[j, left : 2 * left, :]
                    conv_in[code - 1, 0 : 1 + tail, :] = bundle_ref[
                        j, 2 * left : 2 * left + 1 + tail, :
                    ].astype(F32)

        for p in range(peers):
            for g in range(groups):
                gathered[p * group_rows : (p + 1) * group_rows, g * LANES : (g + 1) * LANES] = recv_ref[
                    p * block_rows + g * group_rows : p * block_rows + (g + 1) * group_rows, :
                ]
        codes = jnp.concatenate(
            [recv_ref[(p + 1) * block_rows - TILE : (p + 1) * block_rows, :] for p in range(peers)],
            axis=0,
        )
        spread_lane = ones_where(
            iota((LANES, packed_rows), 1) % group_rows == iota((LANES, packed_rows), 0)
        )
        spread = matmul(codes, spread_lane)
        column = iota((peers * TILE, packed_rows), 1)
        own_tile = iota((peers * TILE, packed_rows), 0) == column // group_rows * TILE
        position = jnp.sum(jnp.where(own_tile, spread, 0.0), axis=0, keepdims=True).astype(I32)
        out_row = iota((row_count, packed_rows), 0) + 1
        column_half = iota((row_count, packed_rows), 1) % group_rows // slots
        hit = out_row == position
        place = jnp.concatenate([ones_where(hit & (column_half == h)) for h in range(FOLD)], axis=0)
        halves = matmul(place, gathered[...])
        owned = jnp.concatenate(
            [halves[h * row_count : (h + 1) * row_count, :] for h in range(FOLD)], axis=1
        )
        centered = owned - jnp.mean(owned, axis=-1, keepdims=True)
        spread_of = jnp.mean(centered * centered, axis=-1, keepdims=True)
        normed = (centered * lax.rsqrt(spread_of + EPSILON)).astype(BF16)
        qkv = matmul(normed, weight_ref[...]).astype(BF16)

        head_rows = heads * span
        lane_head = iota((head_rows, width), 1) // HEAD
        head_mask = ones_where(lane_head == iota((head_rows, width), 0) // span)
        t_of = iota((head_rows, keys), 0) % span
        key_of = iota((head_rows, keys), 1) - left
        t_row = iota((span, width), 0)
        lane_head16 = iota((span, width), 1) // HEAD
        pick_row = iota((left, keys), 0)
        pick_col = iota((left, keys), 1)
        conv_row = iota((tail, window), 0)
        conv_col = iota((tail, window), 1)
        for s in range(streams):
            valid = valid_ref[s]
            row = slice(s * span, (s + 1) * span)
            keys_all[s, left:keys, :] = qkv[row, width : 2 * width]
            values_all[s, left:keys, :] = qkv[row, 2 * width : 3 * width]
            queries = jnp.concatenate([qkv[row, 0:width]] * heads, axis=0) * head_mask
            scores = matmul_nt(queries, keys_all[s]) * HEAD ** (-0.5)
            allowed = (key_of < 0) | ((key_of <= t_of) & (key_of < valid))
            scores = jnp.where(allowed, scores, -1e30)
            weights = jnp.exp(scores - jnp.max(scores, axis=-1, keepdims=True))
            probabilities = (weights / jnp.sum(weights, axis=-1, keepdims=True)).astype(BF16)
            mixed = matmul(probabilities, values_all[s])
            attended = mixed[0:span, :]
            for h in range(1, heads):
                attended = jnp.where(lane_head16 == h, mixed[h * span : (h + 1) * span, :], attended)
            attended = jnp.where(t_row < valid, attended, 0.0).astype(BF16)
            conv_in[s, 1 + tail : window, :] = attended.astype(F32)
            pick = ones_where(pick_col == pick_row + valid)
            keys_next_ref[s] = matmul(pick, keys_all[s]).astype(BF16)
            values_next_ref[s] = matmul(pick, values_all[s]).astype(BF16)
            conv_pick = ones_where(conv_col == conv_row + (valid + 1))
            conv_next_ref[s] = matmul(conv_pick, conv_in[s].astype(BF16)).astype(BF16)

        taps_f32[...] = taps_ref[...].astype(F32)
        stream_of = iota((streams, LANES), 0)
        valid_rows = jnp.zeros((streams, LANES), I32)
        for s in range(streams):
            valid_rows = jnp.where(stream_of == s, valid_ref[s], valid_rows)
        for c in range(width // LANES):
            lanes = slice(c * LANES, (c + 1) * LANES)
            inputs = [conv_in[:, 1 + j, lanes] for j in range(tail + span)]
            for t in range(span):
                total = inputs[tail + t]
                for i in range(taps):
                    total = total + taps_f32[i : i + 1, lanes] * inputs[t + i]
                encoded_f32[:, t, lanes] = jnp.where(t < valid_rows, total, 0.0)
        encoded_ref[...] = encoded_f32[...].reshape(row_count, width).astype(BF16)

    out_shape = (
        jax.ShapeDtypeStruct((row_count, width), BF16),
        jax.ShapeDtypeStruct((streams, left, width), BF16),
        jax.ShapeDtypeStruct((streams, left, width), BF16),
        jax.ShapeDtypeStruct((streams, tail, width), BF16),
    )
    return pl.pallas_call(
        body,
        out_shape=out_shape,
        in_specs=whole(*[pltpu.SMEM] * 3, *[pltpu.VMEM] * 8),
        out_specs=whole(*[pltpu.VMEM] * 4),
        scratch_shapes=[
            pltpu.VMEM((packed_rows, half), BF16),
            pltpu.VMEM((streams, keys, width), BF16),
            pltpu.VMEM((streams, keys, width), BF16),
            pltpu.VMEM((streams, window, width), F32),
            pltpu.VMEM((taps, width), F32),
            pltpu.VMEM((streams, span, width), F32),
        ],
        name="stream_step",
    )(
        destination, own_index(), valid_count, received, from_lower, from_upper, key_cache,
        value_cache, conv_state, qkv_weight, conv_kernel,
    )


def from_behind(block, axis, distance):
    count = lax.axis_size(axis)
    return lax.ppermute(block, axis, [((i - distance) % count, i) for i in range(count)])


def local(
    frames, route_peer, route_pos, destination, valid_count, key_cache, value_cache, conv_state,
    qkv_weight, conv_kernel,
):
    peers = lax.axis_size("streams")
    row_count = frames.shape[0]
    per_peer = row_count // peers
    capacity = per_peer + per_peer // 2
    up, down = pack_streams(destination, key_cache, value_cache, conv_state, peers)
    from_lower = from_behind(up, "streams", 1)
    from_upper = from_behind(down, "streams", -1)
    packed = pack_frames(frames, route_peer, route_pos, peers, capacity)
    received = lax.all_to_all(packed, "streams", split_axis=0, concat_axis=0, tiled=True)
    return stream_step(
        received, from_lower, from_upper, destination, valid_count, key_cache, value_cache,
        conv_state, qkv_weight, conv_kernel, peers, row_count, capacity,
    )


def solution(mesh):
    rows = P(("groups", "streams"))
    return jax.shard_map(
        local,
        mesh=mesh,
        in_specs=(rows,) * 8 + (P(), P()),
        out_specs=(rows,) * 4,
        check_vma=False,
    )
```

```python
import jax
import jax.numpy as jnp
from jax import lax
from jax.experimental import pallas as pl
from jax.experimental.pallas import tpu as pltpu
from jax.sharding import PartitionSpec as P


HEAD = 96
MIG = 4
EPSILON = 1e-05
LANES = 128
TILE = 8
FOLD = 2

BF16 = jnp.bfloat16
F32 = jnp.float32
I32 = jnp.int32


def iota(shape, axis):
    return lax.broadcasted_iota(I32, shape, axis)


def ones_where(condition):
    return jnp.where(condition, 1.0, 0.0).astype(BF16)


def matmul(left, right):
    return jnp.dot(left, right, preferred_element_type=F32)


def matmul_nt(left, right):
    return lax.dot_general(left, right, (((1,), (1,)), ((), ())), preferred_element_type=F32)


def in_vmem(array):
    return pltpu.with_memory_space_constraint(array, pltpu.VMEM)


def in_hbm(array):
    return pltpu.with_memory_space_constraint(array, pltpu.HBM)


def round_up(value, multiple):
    return -(-value // multiple) * multiple


def whole(*spaces):
    return [pl.BlockSpec(memory_space=space) for space in spaces]


def block_sizes(width, capacity):
    slots = round_up(capacity, TILE // FOLD)
    group_rows = FOLD * slots
    groups = width // FOLD // LANES
    return slots, group_rows, groups, groups * group_rows + TILE


def pack_frames(frames, route_peer, route_pos, peers, capacity):
    row_count, width = frames.shape
    slots, group_rows, groups, block_rows = block_sizes(width, capacity)
    half = width // FOLD

    def body(frames_ref, peer_ref, pos_ref, out_ref):
        peer = peer_ref[...]
        owner = ones_where(iota((peers, row_count), 0) == peer)
        earlier = ones_where(iota((row_count, row_count), 0) < iota((row_count, row_count), 1))
        running = matmul(owner, earlier)
        slot = jnp.sum(running * owner.astype(F32), axis=0, keepdims=True).astype(I32)
        flat = peer * group_rows + slot
        rows = iota((peers * group_rows, row_count), 0)
        pick = jnp.concatenate([ones_where(rows == flat + h * slots) for h in range(FOLD)], axis=1)
        source = jnp.concatenate(
            [frames_ref[:, h * half : (h + 1) * half] for h in range(FOLD)], axis=0
        )
        packed = matmul(pick, source).astype(BF16)
        owner_tile = ones_where(iota((peers * TILE, row_count), 0) // TILE == peer)
        lane = iota((LANES, row_count), 0)
        in_lane = (lane % slots == slot) & (lane < group_rows)
        code = jnp.where(in_lane, (pos_ref[...] + 1).astype(F32), 0.0).astype(BF16)
        codes = matmul_nt(owner_tile, code).astype(BF16)
        for p in range(peers):
            for g in range(groups):
                out_ref[p * block_rows + g * group_rows : p * block_rows + (g + 1) * group_rows, :] = (
                    packed[p * group_rows : (p + 1) * group_rows, g * LANES : (g + 1) * LANES]
                )
            out_ref[(p + 1) * block_rows - TILE : (p + 1) * block_rows, :] = codes[
                p * TILE : (p + 1) * TILE, :
            ]

    return pl.pallas_call(
        body,
        out_shape=jax.ShapeDtypeStruct((peers * block_rows, LANES), BF16),
        in_specs=whole(pltpu.VMEM, pltpu.VMEM, pltpu.VMEM),
        out_specs=pl.BlockSpec(memory_space=pltpu.VMEM),
        compiler_params=pltpu.CompilerParams(vmem_limit_bytes=12 << 20),
        name="pack_frames",
    )(in_hbm(frames), in_hbm(route_peer.reshape(1, -1)), in_hbm(route_pos.reshape(1, -1)))


def pack_streams(destination, key_cache, value_cache, conv_state, peers):
    streams, left, width = key_cache.shape
    tail = conv_state.shape[0]
    rows = 2 * left + 1 + tail

    def body(dest_ref, own_ref, key_ref, value_ref, conv_ref, up_ref, down_ref, conv_f32):
        own = own_ref[0]
        conv_f32[...] = conv_ref[...].astype(F32)
        up_ref[...] = jnp.zeros_like(up_ref)
        down_ref[...] = jnp.zeros_like(down_ref)

        def put(out_ref, rank, j, slot):
            out_ref[rank, 0:left, :] = key_ref[j]
            out_ref[rank, left : 2 * left, :] = value_ref[j]
            code = jnp.full((1, width), slot + 1, I32).astype(F32)
            out_ref[rank, 2 * left : rows, :] = jnp.concatenate(
                [code, conv_f32[:, j, :]], axis=0
            ).astype(BF16)

        def step(chosen_device, out_ref):
            rank = jnp.int32(0)
            for j in range(streams):
                target = dest_ref[j]
                chosen = target // streams == chosen_device

                @pl.when(chosen)
                def _():
                    put(out_ref, jnp.minimum(rank, MIG - 1), j, target % streams)

                rank = rank + chosen.astype(I32)

        step((own + 1) % peers, up_ref)
        step((own + peers - 1) % peers, down_ref)

    bundle = jax.ShapeDtypeStruct((MIG, rows, width), BF16)
    return pl.pallas_call(
        body,
        out_shape=(bundle, bundle),
        in_specs=whole(pltpu.SMEM, pltpu.SMEM, pltpu.VMEM, pltpu.VMEM, pltpu.VMEM),
        out_specs=whole(pltpu.VMEM, pltpu.VMEM),
        scratch_shapes=[pltpu.VMEM((tail, streams, width), F32)],
        compiler_params=pltpu.CompilerParams(vmem_limit_bytes=12 << 20),
        name="pack_streams",
    )(*map(in_hbm, (destination, own_index(), key_cache, value_cache, conv_state)))


def own_index():
    return lax.axis_index("streams").astype(I32).reshape(1)


def settle_streams(
    from_lower, from_upper, destination, valid_count, key_cache, value_cache, conv_state,
    qkv_weight, conv_kernel, span,
):
    streams, left, width = key_cache.shape
    tail = conv_state.shape[0]
    taps = conv_kernel.shape[0]
    model = qkv_weight.shape[0]

    def body(
        dest_ref, own_ref, valid_ref, lower_ref, upper_ref, key_ref, value_ref, conv_ref, taps_ref,
        weight_hbm, keys_old, values_old, keys_next, values_next, conv_next, conv_part, weight_ref,
        conv_in, conv_f32, taps_f32, sem,
    ):
        weight_copy = pltpu.make_async_copy(weight_hbm.at[:, 0:width], weight_ref, sem)
        weight_copy.start()
        own = own_ref[0]
        codes = [
            (bundle_ref, j, jnp.max(bundle_ref[j, 2 * left : 2 * left + 1, :].astype(F32)).astype(I32))
            for bundle_ref in (lower_ref, upper_ref)
            for j in range(MIG)
        ]
        taps_f32[...] = taps_ref[...].astype(F32)
        conv_f32[...] = conv_ref[...].astype(F32)
        for j in range(streams):
            target = dest_ref[j]

            @pl.when(target // streams == own)
            def _():
                slot = target % streams
                keys_old[slot] = key_ref[j]
                values_old[slot] = value_ref[j]
                conv_in[slot, 1 : 1 + tail, :] = conv_f32[:, j, :]

        for bundle_ref, j, code in codes:

            @pl.when(code > 0)
            def _():
                keys_old[code - 1] = bundle_ref[j, 0:left, :]
                values_old[code - 1] = bundle_ref[j, left : 2 * left, :]
                conv_in[code - 1] = bundle_ref[j, 2 * left : 2 * left + 1 + tail, :].astype(F32)

        conv_in[:, 0:1, :] = jnp.zeros((streams, 1, width), F32)
        pick_row = iota((left, left), 0)
        pick_col = iota((left, left), 1)
        conv_row = iota((tail, 1 + tail), 0)
        conv_col = iota((tail, 1 + tail), 1)
        for s in range(streams):
            valid = valid_ref[s]
            pick = ones_where(pick_col == pick_row + valid)
            keys_next[s] = matmul(pick, keys_old[s]).astype(BF16)
            values_next[s] = matmul(pick, values_old[s]).astype(BF16)
            conv_pick = ones_where(conv_col == conv_row + (valid + 1))
            conv_f32[:, s, :] = matmul(conv_pick, conv_in[s].astype(BF16))
        conv_next[...] = conv_f32[...].astype(BF16)
        for c in range(width // LANES):
            lanes = slice(c * LANES, (c + 1) * LANES)
            inputs = [conv_in[:, 1 + j, lanes] for j in range(tail)]
            for t in range(span):
                total = jnp.zeros((streams, LANES), F32)
                for i in range(min(taps, tail - t)):
                    total = total + taps_f32[i : i + 1, lanes] * inputs[t + i]
                conv_part[t, :, lanes] = total
        weight_copy.wait()

    cache = pltpu.HBM(key_cache.shape, BF16)
    return pl.pallas_call(
        body,
        out_shape=(
            cache, cache, cache, cache,
            pltpu.HBM(conv_state.shape, BF16),
            pltpu.HBM((span, streams, width), F32),
            pltpu.VMEM((model, width), BF16),
        ),
        in_specs=whole(*[pltpu.SMEM] * 3, *[pltpu.VMEM] * 6, pl.ANY),
        out_specs=whole(*[pltpu.VMEM] * 7),
        scratch_shapes=[
            pltpu.VMEM((streams, 1 + tail, width), F32),
            pltpu.VMEM((tail, streams, width), F32),
            pltpu.VMEM((taps, width), F32),
            pltpu.SemaphoreType.DMA,
        ],
        compiler_params=pltpu.CompilerParams(vmem_limit_bytes=24 << 20),
        name="settle_streams",
    )(
        *map(
            in_hbm,
            (
                destination, own_index(), valid_count, from_lower, from_upper, key_cache,
                value_cache, conv_state, conv_kernel, qkv_weight,
            ),
        )
    )


def stream_step(received, valid_count, settled, qkv_weight, conv_kernel, peers, row_count, capacity):
    keys_old, values_old, keys_kept, values_kept, conv_kept, conv_part, first_weight = settled
    streams, left, width = keys_old.shape
    tail = conv_kept.shape[0]
    taps = conv_kernel.shape[0]
    span = row_count // streams
    model = qkv_weight.shape[0]
    half = model // FOLD
    heads = width // HEAD
    keys = left + span
    slots, group_rows, groups, block_rows = block_sizes(model, capacity)
    packed_rows = peers * group_rows

    def body(
        valid_ref, recv_ref, first_ref, key_hbm, value_hbm, keys_kept_hbm, values_kept_hbm,
        conv_kept_hbm, conv_part_hbm, weight_hbm, taps_hbm, encoded_hbm, keys_next_hbm,
        values_next_hbm, conv_next_hbm,
        keys_all, values_all, keys_kept_ref, values_kept_ref, conv_kept_ref, conv_part_ref,
        weight_ref, taps_ref, encoded_ref, keys_next_ref, values_next_ref, conv_next_ref,
        gathered, attended_all, attended_f32, taps_f32, encoded_f32, in_sems, weight_sems, out_sems,
    ):
        weight_copies = [
            pltpu.make_async_copy(
                weight_hbm.at[:, (c + 1) * width : (c + 2) * width],
                weight_ref.at[c],
                weight_sems.at[c],
            )
            for c in range(2)
        ]
        in_copies = [
            pltpu.make_async_copy(source, target, in_sems.at[n])
            for n, (source, target) in enumerate(
                (
                    (key_hbm, keys_all.at[:, 0:left, :]),
                    (value_hbm, values_all.at[:, 0:left, :]),
                    (keys_kept_hbm, keys_kept_ref),
                    (values_kept_hbm, values_kept_ref),
                    (conv_kept_hbm, conv_kept_ref),
                    (conv_part_hbm, conv_part_ref),
                    (taps_hbm, taps_ref),
                )
            )
        ]
        out_copies = [
            pltpu.make_async_copy(source, target, out_sems.at[n])
            for n, (source, target) in enumerate(
                (
                    (encoded_ref, encoded_hbm), (keys_next_ref, keys_next_hbm),
                    (values_next_ref, values_next_hbm), (conv_next_ref, conv_next_hbm),
                )
            )
        ]
        for copy in weight_copies + in_copies:
            copy.start()

        for p in range(peers):
            for g in range(groups):
                gathered[p * group_rows : (p + 1) * group_rows, g * LANES : (g + 1) * LANES] = recv_ref[
                    p * block_rows + g * group_rows : p * block_rows + (g + 1) * group_rows, :
                ]
        codes = jnp.concatenate(
            [recv_ref[(p + 1) * block_rows - TILE : (p + 1) * block_rows, :] for p in range(peers)],
            axis=0,
        )
        spread_lane = ones_where(
            iota((LANES, packed_rows), 1) % group_rows == iota((LANES, packed_rows), 0)
        )
        spread = matmul(codes, spread_lane)
        column = iota((peers * TILE, packed_rows), 1)
        own_tile = iota((peers * TILE, packed_rows), 0) == column // group_rows * TILE
        position = jnp.sum(jnp.where(own_tile, spread, 0.0), axis=0, keepdims=True).astype(I32)
        out_row = iota((row_count, packed_rows), 0) + 1
        column_half = iota((row_count, packed_rows), 1) % group_rows // slots
        hit = out_row == position
        place = jnp.concatenate([ones_where(hit & (column_half == h)) for h in range(FOLD)], axis=0)
        halves = matmul(place, gathered[...])
        owned = jnp.concatenate(
            [halves[h * row_count : (h + 1) * row_count, :] for h in range(FOLD)], axis=1
        )
        centered = owned - jnp.mean(owned, axis=-1, keepdims=True)
        spread_of = jnp.mean(centered * centered, axis=-1, keepdims=True)
        normed = (centered * lax.rsqrt(spread_of + EPSILON)).astype(BF16)
        queries_new = matmul(normed, first_ref[...]).astype(BF16)
        weight_copies[0].wait()
        keys_new = matmul(normed, weight_ref[0]).astype(BF16)
        weight_copies[1].wait()
        values_new = matmul(normed, weight_ref[1]).astype(BF16)
        for copy in in_copies:
            copy.wait()

        def new_rows(row_stream, row_index, kept):
            column = iota(row_stream.shape, 1)
            valid = jnp.zeros(row_stream.shape, I32)
            for s in range(streams):
                valid = jnp.where(row_stream == s, valid_ref[s], valid)
            frame = row_index + valid - kept
            return ones_where((frame >= 0) & (column == row_stream * span + frame))

        row = iota((streams * left, row_count), 0)
        cache_pick = new_rows(row // left, row % left, left)
        cache_shape = (streams, left, width)
        keys_next_ref[...] = (
            keys_kept_ref[...].astype(F32) + matmul(cache_pick, keys_new).reshape(cache_shape)
        ).astype(BF16)
        values_next_ref[...] = (
            values_kept_ref[...].astype(F32) + matmul(cache_pick, values_new).reshape(cache_shape)
        ).astype(BF16)
        out_copies[1].start()
        out_copies[2].start()

        head_rows = heads * span
        head_mask = ones_where(
            iota((head_rows, width), 1) // HEAD == iota((head_rows, width), 0) // span
        )
        t_of = iota((keys, head_rows), 1) % span
        key_of = iota((keys, head_rows), 0) - left
        t_row = iota((span, width), 0)
        lane_head = iota((span, width), 1) // HEAD
        for s in range(streams):
            valid = valid_ref[s]
            rows = slice(s * span, (s + 1) * span)
            keys_all[s, left:keys, :] = keys_new[rows, :]
            values_all[s, left:keys, :] = values_new[rows, :]
            queries = jnp.concatenate([queries_new[rows, :]] * heads, axis=0) * head_mask
            scores = matmul_nt(keys_all[s], queries) * HEAD ** (-0.5)
            allowed = (key_of < 0) | ((key_of <= t_of) & (key_of < valid))
            scores = jnp.where(allowed, scores, -1e30)
            weights = jnp.exp(scores - jnp.max(scores, axis=0, keepdims=True))
            probabilities = (weights / jnp.sum(weights, axis=0, keepdims=True)).astype(BF16)
            mixed = lax.dot_general(
                probabilities, values_all[s], (((0,), (0,)), ((), ())), preferred_element_type=F32
            )
            attended = mixed[0:span, :]
            for h in range(1, heads):
                attended = jnp.where(lane_head == h, mixed[h * span : (h + 1) * span, :], attended)
            attended = jnp.where(t_row < valid, attended, 0.0).astype(BF16)
            attended_all[rows, :] = attended
            attended_f32[s] = attended.astype(F32)

        row = iota((tail * streams, row_count), 0)
        conv_pick = new_rows(row % streams, row // streams, tail)
        conv_next_ref[...] = (
            conv_kept_ref[...].astype(F32)
            + matmul(conv_pick, attended_all[...]).reshape(tail, streams, width)
        ).astype(BF16)
        out_copies[3].start()

        taps_f32[...] = taps_ref[...].astype(F32)
        stream_of = iota((streams, LANES), 0)
        valid_rows = jnp.zeros((streams, LANES), I32)
        for s in range(streams):
            valid_rows = jnp.where(stream_of == s, valid_ref[s], valid_rows)
        for c in range(width // LANES):
            lanes = slice(c * LANES, (c + 1) * LANES)
            inputs = [attended_f32[:, t, lanes] for t in range(span)]
            for t in range(span):
                total = conv_part_ref[t, :, lanes] + inputs[t]
                for i in range(max(tail - t, 0), taps):
                    total = total + taps_f32[i : i + 1, lanes] * inputs[t + i - tail]
                encoded_f32[:, t, lanes] = jnp.where(t < valid_rows, total, 0.0)
        encoded_ref[...] = encoded_f32[...].reshape(row_count, width).astype(BF16)
        out_copies[0].start()
        for copy in out_copies:
            copy.wait()

    encoded_shape = (row_count, width)
    cache_shape = (streams, left, width)
    conv_shape = (tail, streams, width)
    out_shapes = (encoded_shape, cache_shape, cache_shape, conv_shape)
    return pl.pallas_call(
        body,
        out_shape=[jax.ShapeDtypeStruct(shape, BF16) for shape in out_shapes],
        in_specs=whole(pltpu.SMEM, *[pltpu.VMEM] * 2, *[pl.ANY] * 8),
        out_specs=whole(*[pl.ANY] * 4),
        scratch_shapes=[
            pltpu.VMEM((streams, keys, width), BF16),
            pltpu.VMEM((streams, keys, width), BF16),
            pltpu.VMEM(cache_shape, BF16),
            pltpu.VMEM(cache_shape, BF16),
            pltpu.VMEM(conv_shape, BF16),
            pltpu.VMEM((span, streams, width), F32),
            pltpu.VMEM((2, model, width), BF16),
            pltpu.VMEM((taps, width), BF16),
            *[pltpu.VMEM(shape, BF16) for shape in out_shapes],
            pltpu.VMEM((packed_rows, half), BF16),
            pltpu.VMEM((row_count, width), BF16),
            pltpu.VMEM((streams, span, width), F32),
            pltpu.VMEM((taps, width), F32),
            pltpu.VMEM((streams, span, width), F32),
            pltpu.SemaphoreType.DMA((7,)),
            pltpu.SemaphoreType.DMA((2,)),
            pltpu.SemaphoreType.DMA((4,)),
        ],
        compiler_params=pltpu.CompilerParams(vmem_limit_bytes=32 << 20),
        name="stream_step",
    )(
        in_hbm(valid_count), in_vmem(received), in_vmem(first_weight),
        *map(
            in_hbm,
            (
                keys_old, values_old, keys_kept, values_kept, conv_kept, conv_part, qkv_weight,
                conv_kernel,
            ),
        ),
    )


def from_behind(block, axis, distance):
    count = lax.axis_size(axis)
    return lax.ppermute(block, axis, [((i - distance) % count, i) for i in range(count)])


def local(
    frames, route_peer, route_pos, destination, valid_count, key_cache, value_cache, conv_state,
    qkv_weight, conv_kernel,
):
    peers = lax.axis_size("streams")
    row_count = frames.shape[0]
    per_peer = row_count // peers
    capacity = per_peer + per_peer // 2
    conv_by_time = conv_state.transpose(1, 0, 2)
    up, down = pack_streams(destination, key_cache, value_cache, conv_by_time, peers)
    from_lower = from_behind(up, "streams", 1)
    from_upper = from_behind(down, "streams", -1)
    packed = pack_frames(frames, route_peer, route_pos, peers, capacity)
    received = lax.all_to_all(packed, "streams", split_axis=0, concat_axis=0, tiled=True)
    settled = settle_streams(
        from_lower, from_upper, destination, valid_count, key_cache, value_cache,
        conv_by_time, qkv_weight, conv_kernel, row_count // key_cache.shape[0],
    )
    encoded, keys_next, values_next, conv_next = stream_step(
        received, valid_count, settled, qkv_weight, conv_kernel, peers, row_count, capacity
    )
    return encoded, keys_next, values_next, conv_next.transpose(1, 0, 2)


def solution(mesh):
    rows = P(("groups", "streams"))
    return jax.shard_map(
        local,
        mesh=mesh,
        in_specs=(rows,) * 8 + (P(), P()),
        out_specs=(rows,) * 4,
        check_vma=False,
    )
```

```python
import jax
import jax.numpy as jnp
from jax import lax
from jax.experimental import pallas as pl
from jax.experimental.pallas import tpu as pltpu
from jax.sharding import PartitionSpec as P


HEAD = 96
MIG = 4
EPSILON = 1e-05
LANES = 128
TILE = 8
FOLD = 2
CHUNKS = 3

BF16 = jnp.bfloat16
F32 = jnp.float32
I32 = jnp.int32


def iota(shape, axis):
    return lax.broadcasted_iota(I32, shape, axis)


def ones_where(condition):
    return jnp.where(condition, 1.0, 0.0).astype(BF16)


def matmul(left, right):
    return jnp.dot(left, right, preferred_element_type=F32)


def matmul_nt(left, right):
    return lax.dot_general(left, right, (((1,), (1,)), ((), ())), preferred_element_type=F32)


def in_vmem(array):
    return pltpu.with_memory_space_constraint(array, pltpu.VMEM)


def in_hbm(array):
    return pltpu.with_memory_space_constraint(array, pltpu.HBM)


def round_up(value, multiple):
    return -(-value // multiple) * multiple


def whole(*spaces):
    return [pl.BlockSpec(memory_space=space) for space in spaces]


def block_sizes(width, capacity):
    slots = round_up(capacity, TILE // FOLD)
    group_rows = FOLD * slots
    groups = width // FOLD // LANES
    return slots, group_rows, groups, groups * group_rows + TILE


def pack_all(
    frames, route_peer, route_pos, destination, key_cache, value_cache, conv_state, peers, capacity
):
    row_count, model = frames.shape
    slots, group_rows, groups, block_rows = block_sizes(model, capacity)
    half = model // FOLD
    streams, left, width = key_cache.shape
    tail = conv_state.shape[0]
    rows = 2 * left + 1 + tail

    def body(
        dest_ref, own_ref, peer_ref, pos_ref, key_hbm, value_hbm, conv_hbm, frames_hbm,
        packed_ref, up_ref, down_ref, key_ref, value_ref, conv_ref, frames_ref, conv_f32, sems,
    ):
        copies = [
            pltpu.make_async_copy(source, target, sems.at[n])
            for n, (source, target) in enumerate(
                (
                    (frames_hbm, frames_ref), (conv_hbm, conv_ref), (key_hbm, key_ref),
                    (value_hbm, value_ref),
                )
            )
        ]
        for copy in copies:
            copy.start()
        own = own_ref[0]
        peer = peer_ref[...]
        owner = ones_where(iota((peers, row_count), 0) == peer)
        earlier = ones_where(iota((row_count, row_count), 0) < iota((row_count, row_count), 1))
        running = matmul(owner, earlier)
        slot = jnp.sum(running * owner.astype(F32), axis=0, keepdims=True).astype(I32)
        flat = peer * group_rows + slot
        packed_row = iota((peers * group_rows, row_count), 0)
        pick = jnp.concatenate(
            [ones_where(packed_row == flat + h * slots) for h in range(FOLD)], axis=1
        )
        owner_tile = ones_where(iota((peers * TILE, row_count), 0) // TILE == peer)
        lane = iota((LANES, row_count), 0)
        in_lane = (lane % slots == slot) & (lane < group_rows)
        code = jnp.where(in_lane, (pos_ref[...] + 1).astype(F32), 0.0).astype(BF16)
        codes = matmul_nt(owner_tile, code).astype(BF16)
        copies[0].wait()
        source = jnp.concatenate(
            [frames_ref[:, h * half : (h + 1) * half] for h in range(FOLD)], axis=0
        )
        packed = matmul(pick, source).astype(BF16)
        for p in range(peers):
            for g in range(groups):
                first = p * block_rows + g * group_rows
                packed_ref[first : first + group_rows, :] = packed[
                    p * group_rows : (p + 1) * group_rows, g * LANES : (g + 1) * LANES
                ]
            packed_ref[(p + 1) * block_rows - TILE : (p + 1) * block_rows, :] = codes[
                p * TILE : (p + 1) * TILE, :
            ]
        copies[1].wait()
        conv_f32[...] = conv_ref[...].astype(F32)
        copies[2].wait()
        copies[3].wait()

        def put(out_ref, rank, j, slot):
            out_ref[rank, 0:left, :] = key_ref[j]
            out_ref[rank, left : 2 * left, :] = value_ref[j]
            code = jnp.full((1, width), slot + 1, I32).astype(F32)
            out_ref[rank, 2 * left : rows, :] = jnp.concatenate(
                [code, conv_f32[:, j, :]], axis=0
            ).astype(BF16)

        for out_ref, chosen_device in (
            (up_ref, (own + 1) % peers), (down_ref, (own + peers - 1) % peers),
        ):
            out_ref[:, 2 * left : rows, :] = jnp.zeros((MIG, 1 + tail, width), BF16)
            rank = jnp.int32(0)
            for j in range(streams):
                target = dest_ref[j]
                chosen = target // streams == chosen_device

                @pl.when(chosen)
                def _():
                    put(out_ref, jnp.minimum(rank, MIG - 1), j, target % streams)

                rank = rank + chosen.astype(I32)

    bundle = pltpu.VMEM((MIG, rows, width), BF16)
    return pl.pallas_call(
        body,
        out_shape=(pltpu.VMEM((peers * block_rows, LANES), BF16), bundle, bundle),
        in_specs=whole(*[pltpu.SMEM] * 2, *[pltpu.VMEM] * 2, *[pl.ANY] * 4),
        out_specs=whole(*[pltpu.VMEM] * 3),
        scratch_shapes=[
            pltpu.VMEM(key_cache.shape, BF16),
            pltpu.VMEM(key_cache.shape, BF16),
            pltpu.VMEM(conv_state.shape, BF16),
            pltpu.VMEM(frames.shape, BF16),
            pltpu.VMEM(conv_state.shape, F32),
            pltpu.SemaphoreType.DMA((4,)),
        ],
        compiler_params=pltpu.CompilerParams(vmem_limit_bytes=12 << 20),
        name="pack_all",
    )(
        *map(
            in_hbm,
            (
                destination, own_index(), route_peer.reshape(1, -1), route_pos.reshape(1, -1),
                key_cache, value_cache, conv_state, frames,
            ),
        )
    )


def own_index():
    return lax.axis_index("streams").astype(I32).reshape(1)


def settle_streams(
    from_lower, from_upper, destination, key_cache, value_cache, conv_state, conv_kernel
):
    streams, left, width = key_cache.shape
    tail = conv_state.shape[0]
    cache = (streams, left, width)

    def body(
        dest_ref, own_ref, lower_ref, upper_ref, key_hbm, value_hbm, conv_hbm, taps_hbm,
        keys_old, values_old, conv_old, taps_f32,
        key_ref, value_ref, conv_ref, taps_ref, conv_f32, sems,
    ):
        copies = [
            pltpu.make_async_copy(source, target, sems.at[n])
            for n, (source, target) in enumerate(
                (
                    (conv_hbm, conv_ref), (key_hbm, key_ref), (value_hbm, value_ref),
                    (taps_hbm, taps_ref),
                )
            )
        ]
        for copy in copies:
            copy.start()
        own = own_ref[0]
        codes = [
            (bundle_ref, j, jnp.max(bundle_ref[j, 2 * left : 2 * left + 1, :].astype(F32)).astype(I32))
            for bundle_ref in (lower_ref, upper_ref)
            for j in range(MIG)
        ]
        for bundle_ref, j, code in codes:

            @pl.when(code > 0)
            def _():
                keys_old[code - 1] = bundle_ref[j, 0:left, :]
                values_old[code - 1] = bundle_ref[j, left : 2 * left, :]
                conv_old[code - 1] = bundle_ref[j, 2 * left : 2 * left + 1 + tail, :].astype(F32)

        for copy in copies:
            copy.wait()
        taps_f32[...] = taps_ref[...].astype(F32)
        conv_f32[...] = conv_ref[...].astype(F32)
        for j in range(streams):
            target = dest_ref[j]

            @pl.when(target // streams == own)
            def _():
                slot = target % streams
                keys_old[slot] = key_ref[j]
                values_old[slot] = value_ref[j]
                conv_old[slot, 1 : 1 + tail, :] = conv_f32[:, j, :]

        conv_old[:, 0:1, :] = jnp.zeros((streams, 1, width), F32)

    return pl.pallas_call(
        body,
        out_shape=(
            pltpu.VMEM(cache, BF16),
            pltpu.VMEM(cache, BF16),
            pltpu.VMEM((streams, 1 + tail, width), F32),
            pltpu.VMEM(conv_kernel.shape, F32),
        ),
        in_specs=whole(*[pltpu.SMEM] * 2, *[pltpu.VMEM] * 2, *[pl.ANY] * 4),
        out_specs=whole(*[pltpu.VMEM] * 4),
        scratch_shapes=[
            pltpu.VMEM(cache, BF16),
            pltpu.VMEM(cache, BF16),
            pltpu.VMEM(conv_state.shape, BF16),
            pltpu.VMEM(conv_kernel.shape, BF16),
            pltpu.VMEM(conv_state.shape, F32),
            pltpu.SemaphoreType.DMA((4,)),
        ],
        compiler_params=pltpu.CompilerParams(vmem_limit_bytes=16 << 20),
        name="settle_streams",
    )(
        *map(in_hbm, (destination, own_index())), in_vmem(from_lower), in_vmem(from_upper),
        *map(in_hbm, (key_cache, value_cache, conv_state, conv_kernel)),
    )


def stream_step(received, valid_count, settled, qkv_weight, peers, row_count, capacity):
    keys_settled, values_settled, conv_settled, taps_settled = settled
    streams, left, width = keys_settled.shape
    tail = conv_settled.shape[1] - 1
    taps = taps_settled.shape[0]
    span = row_count // streams
    model, columns = qkv_weight.shape
    half = model // FOLD
    chunk = columns // CHUNKS
    heads = width // HEAD
    keys = left + span
    window = 1 + tail + span
    slots, group_rows, groups, block_rows = block_sizes(model, capacity)
    packed_rows = peers * group_rows

    def body(
        valid_ref, recv_ref, keys_old, values_old, conv_old, taps_ref, weight_hbm,
        encoded_hbm, keys_next_hbm, values_next_hbm, conv_next_hbm,
        encoded_ref, keys_next_ref, values_next_ref, conv_next_ref,
        weight_ref, gathered, qkv_ref, attended_f32, conv_part, conv_f32, encoded_f32,
        weight_sems, out_sems,
    ):
        weight_copies = [
            pltpu.make_async_copy(
                weight_hbm.at[:, c * chunk : (c + 1) * chunk], weight_ref.at[c], weight_sems.at[c]
            )
            for c in range(CHUNKS)
        ]
        out_copies = [
            pltpu.make_async_copy(source, target, out_sems.at[n])
            for n, (source, target) in enumerate(
                (
                    (encoded_ref, encoded_hbm), (keys_next_ref, keys_next_hbm),
                    (values_next_ref, values_next_hbm), (conv_next_ref, conv_next_hbm),
                )
            )
        ]
        for copy in weight_copies:
            copy.start()

        for p in range(peers):
            for g in range(groups):
                gathered[p * group_rows : (p + 1) * group_rows, g * LANES : (g + 1) * LANES] = recv_ref[
                    p * block_rows + g * group_rows : p * block_rows + (g + 1) * group_rows, :
                ]
        codes = jnp.concatenate(
            [recv_ref[(p + 1) * block_rows - TILE : (p + 1) * block_rows, :] for p in range(peers)],
            axis=0,
        )
        spread_lane = ones_where(
            iota((LANES, packed_rows), 1) % group_rows == iota((LANES, packed_rows), 0)
        )
        spread = matmul(codes, spread_lane)
        column = iota((peers * TILE, packed_rows), 1)
        own_tile = iota((peers * TILE, packed_rows), 0) == column // group_rows * TILE
        position = jnp.sum(jnp.where(own_tile, spread, 0.0), axis=0, keepdims=True).astype(I32)
        out_row = iota((row_count, packed_rows), 0) + 1
        column_half = iota((row_count, packed_rows), 1) % group_rows // slots
        hit = out_row == position
        place = jnp.concatenate([ones_where(hit & (column_half == h)) for h in range(FOLD)], axis=0)
        halves = matmul(place, gathered[...])
        owned = jnp.concatenate(
            [halves[h * row_count : (h + 1) * row_count, :] for h in range(FOLD)], axis=1
        )
        centered = owned - jnp.mean(owned, axis=-1, keepdims=True)
        spread_of = jnp.mean(centered * centered, axis=-1, keepdims=True)
        normed = (centered * lax.rsqrt(spread_of + EPSILON)).astype(BF16)
        lane_chunks = [slice(c * LANES, (c + 1) * LANES) for c in range(width // LANES)]

        def old_part(lanes):
            inputs = [conv_old[:, 1 + j, lanes] for j in range(tail)]
            for t in range(span):
                total = inputs[t] * taps_ref[0:1, lanes]
                for i in range(1, min(taps, tail - t)):
                    total = total + taps_ref[i : i + 1, lanes] * inputs[t + i]
                conv_part[t, :, lanes] = total

        for c in range(CHUNKS):
            weight_copies[c].wait()
            qkv_ref[:, c * chunk : (c + 1) * chunk] = matmul(normed, weight_ref[c]).astype(BF16)
            for lanes in lane_chunks[c::CHUNKS]:
                old_part(lanes)

        head_rows = heads * span
        head_mask = ones_where(
            iota((head_rows, width), 1) // HEAD == iota((head_rows, width), 0) // span
        )
        t_of = iota((keys, head_rows), 1) % span
        key_of = iota((keys, head_rows), 0) - left
        causal = key_of <= t_of
        t_row = iota((span, LANES), 0)
        lane = iota((span, LANES), 1)
        pick_shift = iota((left, keys), 1) - iota((left, keys), 0)
        conv_shift = iota((tail, window), 1) - iota((tail, window), 0)
        all_rows = [slice(s * span, (s + 1) * span) for s in range(streams)]
        all_keys = []
        all_values = []
        all_scores = []
        for s in range(streams):
            rows = all_rows[s]
            queries = jnp.concatenate([qkv_ref[rows, 0:width]] * heads, axis=0) * head_mask
            all_keys.append(
                jnp.concatenate([keys_old[s], qkv_ref[rows, width : 2 * width]], axis=0)
            )
            all_values.append(
                jnp.concatenate([values_old[s], qkv_ref[rows, 2 * width : 3 * width]], axis=0)
            )
            all_scores.append(matmul_nt(all_keys[s], queries))
        all_probabilities = []
        for s in range(streams):
            allowed = (key_of < 0) | (causal & (key_of < valid_ref[s]))
            scores = jnp.where(allowed, all_scores[s] * HEAD ** (-0.5), -1e30)
            weights = jnp.exp(scores - jnp.max(scores, axis=0, keepdims=True))
            all_probabilities.append(
                (weights / jnp.sum(weights, axis=0, keepdims=True)).astype(BF16)
            )
        for s in range(streams):
            pick = ones_where(pick_shift == valid_ref[s])
            keys_next_ref[s] = matmul(pick, all_keys[s]).astype(BF16)
            values_next_ref[s] = matmul(pick, all_values[s]).astype(BF16)
        out_copies[1].start()
        out_copies[2].start()
        all_mixed = [
            lax.dot_general(
                all_probabilities[s], all_values[s], (((0,), (0,)), ((), ())),
                preferred_element_type=F32,
            )
            for s in range(streams)
        ]
        for s in range(streams):
            for c in range(width // LANES):
                lanes = slice(c * LANES, (c + 1) * LANES)
                first = c * LANES // HEAD
                last = ((c + 1) * LANES - 1) // HEAD
                attended = all_mixed[s][first * span : (first + 1) * span, lanes]
                for h in range(first + 1, last + 1):
                    attended = jnp.where(
                        lane >= h * HEAD - c * LANES,
                        all_mixed[s][h * span : (h + 1) * span, lanes],
                        attended,
                    )
                attended = jnp.where(t_row < valid_ref[s], attended, 0.0).astype(BF16)
                attended_f32[s, :, lanes] = attended.astype(F32)

        for s in range(streams):
            conv_pick = ones_where(conv_shift == valid_ref[s] + 1)
            conv_rows = jnp.concatenate([conv_old[s], attended_f32[s]], axis=0).astype(BF16)
            conv_f32[:, s, :] = matmul(conv_pick, conv_rows)
        conv_next_ref[...] = conv_f32[...].reshape(tail * streams, width).astype(BF16)
        out_copies[3].start()

        stream_of = iota((streams, LANES), 0)
        valid_rows = jnp.zeros((streams, LANES), I32)
        for s in range(streams):
            valid_rows = jnp.where(stream_of == s, valid_ref[s], valid_rows)
        for lanes in lane_chunks:
            inputs = [attended_f32[:, t, lanes] for t in range(span)]
            for t in range(span):
                total = conv_part[t, :, lanes] + inputs[t]
                for i in range(max(tail - t, 0), taps):
                    total = total + taps_ref[i : i + 1, lanes] * inputs[t + i - tail]
                encoded_f32[:, t, lanes] = jnp.where(t < valid_rows, total, 0.0)
        encoded_ref[...] = encoded_f32[...].reshape(row_count, width).astype(BF16)
        out_copies[0].start()
        for copy in out_copies:
            copy.wait()

    cache = (streams, left, width)
    out_shapes = ((row_count, width), cache, cache, (tail * streams, width))
    return pl.pallas_call(
        body,
        out_shape=[jax.ShapeDtypeStruct(shape, BF16) for shape in out_shapes],
        in_specs=whole(pltpu.SMEM, *[pltpu.VMEM] * 5, pl.ANY),
        out_specs=whole(*[pl.ANY] * 4),
        scratch_shapes=[
            *[pltpu.VMEM(shape, BF16) for shape in out_shapes],
            pltpu.VMEM((CHUNKS, model, chunk), BF16),
            pltpu.VMEM((packed_rows, half), BF16),
            pltpu.VMEM((row_count, columns), BF16),
            pltpu.VMEM((streams, span, width), F32),
            pltpu.VMEM((span, streams, width), F32),
            pltpu.VMEM((tail, streams, width), F32),
            pltpu.VMEM((streams, span, width), F32),
            pltpu.SemaphoreType.DMA((CHUNKS,)),
            pltpu.SemaphoreType.DMA((4,)),
        ],
        compiler_params=pltpu.CompilerParams(vmem_limit_bytes=32 << 20),
        name="stream_step",
    )(
        in_hbm(valid_count),
        *map(in_vmem, (received, keys_settled, values_settled, conv_settled, taps_settled)),
        in_hbm(qkv_weight),
    )


def from_behind(block, axis, distance):
    count = lax.axis_size(axis)
    return lax.ppermute(block, axis, [((i - distance) % count, i) for i in range(count)])


def local(
    frames, route_peer, route_pos, destination, valid_count, key_cache, value_cache, conv_state,
    qkv_weight, conv_kernel,
):
    peers = lax.axis_size("streams")
    row_count = frames.shape[0]
    per_peer = row_count // peers
    capacity = per_peer + per_peer // 2
    conv_by_time = conv_state.transpose(1, 0, 2)
    packed, up, down = pack_all(
        frames, route_peer, route_pos, destination, key_cache, value_cache, conv_by_time,
        peers, capacity,
    )
    from_lower = from_behind(up, "streams", 1)
    from_upper = from_behind(down, "streams", -1)
    received = lax.all_to_all(packed, "streams", split_axis=0, concat_axis=0, tiled=True)
    settled = settle_streams(
        from_lower, from_upper, destination, key_cache, value_cache, conv_by_time,
        conv_kernel,
    )
    encoded, keys_next, values_next, conv_next = stream_step(
        received, valid_count, settled, qkv_weight, peers, row_count, capacity
    )
    _, streams, width = conv_by_time.shape
    return (
        encoded, keys_next, values_next,
        conv_next.reshape(-1, streams, width).transpose(1, 0, 2),
    )


def solution(mesh):
    rows = P(("groups", "streams"))
    return jax.shard_map(
        local,
        mesh=mesh,
        in_specs=(rows,) * 8 + (P(), P()),
        out_specs=(rows,) * 4,
        check_vma=False,
    )
```

```python
import jax
import jax.numpy as jnp
from jax import lax
from jax.experimental import pallas as pl
from jax.experimental.pallas import tpu as pltpu
from jax.sharding import PartitionSpec as P


HEAD = 96
MIG = 4
EPSILON = 1e-05
LANES = 128
TILE = 8
FOLD = 2
GROUP = 4
SPLIT = 9
CHUNK_EDGES = (0, 3, 6, 8, 9)
AHEAD = 4

BF16 = jnp.bfloat16
F32 = jnp.float32
I32 = jnp.int32


def iota(shape, axis):
    return lax.broadcasted_iota(I32, shape, axis)


def ones_where(condition):
    return jnp.where(condition, 1.0, 0.0).astype(BF16)


def matmul(left, right):
    return jnp.dot(left, right, preferred_element_type=F32)


def matmul_nt(left, right):
    return lax.dot_general(left, right, (((1,), (1,)), ((), ())), preferred_element_type=F32)


def in_vmem(array):
    return pltpu.with_memory_space_constraint(array, pltpu.VMEM)


def in_hbm(array):
    return pltpu.with_memory_space_constraint(array, pltpu.HBM)


def round_up(value, multiple):
    return -(-value // multiple) * multiple


def whole(*spaces):
    return [pl.BlockSpec(memory_space=space) for space in spaces]


def block_sizes(width, capacity):
    slots = round_up(capacity, TILE // FOLD)
    group_rows = FOLD * slots
    groups = width // FOLD // LANES
    return slots, group_rows, groups, groups * group_rows + TILE


def pack_all(
    frames, route_peer, route_pos, destination, key_cache, value_cache, conv_state, peers, capacity
):
    row_count, model = frames.shape
    slots, group_rows, groups, block_rows = block_sizes(model, capacity)
    half = model // FOLD
    streams, left, width = key_cache.shape
    tail = conv_state.shape[0] // streams
    rows = 2 * left + tail + 1

    def body(
        dest_ref, own_ref, peer_ref, pos_ref, key_hbm, value_hbm, conv_hbm, frames_hbm,
        packed_ref, up_ref, down_ref, conv_ref, frames_ref, conv_f32, sems, move_sems,
    ):
        frames_copy = pltpu.make_async_copy(frames_hbm, frames_ref, sems.at[0])
        conv_copy = pltpu.make_async_copy(conv_hbm, conv_ref, sems.at[1])
        frames_copy.start()
        conv_copy.start()
        own = own_ref[0]
        moves = []
        for n, (out_ref, device) in enumerate(
            ((up_ref, (own + 1) % peers), (down_ref, (own + peers - 1) % peers))
        ):
            rank = jnp.int32(0)
            for j in range(streams):
                target = dest_ref[j]
                chosen = target // streams == device
                place = jnp.minimum(rank, MIG - 1)
                copies = [
                    pltpu.make_async_copy(
                        source.at[j],
                        out_ref.at[place, k * left : (k + 1) * left, :],
                        move_sems.at[n, k, j],
                    )
                    for k, source in enumerate((key_hbm, value_hbm))
                ]

                @pl.when(chosen)
                def _():
                    for copy in copies:
                        copy.start()

                moves.append((out_ref, chosen, place, j, target % streams, copies))
                rank = rank + chosen.astype(I32)

        peer = peer_ref[...]
        owner = ones_where(iota((peers, row_count), 0) == peer)
        earlier = ones_where(iota((row_count, row_count), 0) < iota((row_count, row_count), 1))
        running = matmul(owner, earlier)
        slot = jnp.sum(running * owner.astype(F32), axis=0, keepdims=True).astype(I32)
        flat = peer * group_rows + slot
        packed_row = iota((peers * group_rows, row_count), 0)
        pick = jnp.concatenate(
            [ones_where(packed_row == flat + h * slots) for h in range(FOLD)], axis=1
        )
        owner_tile = ones_where(iota((peers * TILE, row_count), 0) // TILE == peer)
        lane = iota((LANES, row_count), 0)
        in_lane = (lane % slots == slot) & (lane < group_rows)
        code = jnp.where(in_lane, (pos_ref[...] + 1).astype(F32), 0.0).astype(BF16)
        codes = matmul_nt(owner_tile, code).astype(BF16)
        frames_copy.wait()
        source = jnp.concatenate(
            [frames_ref[:, h * half : (h + 1) * half] for h in range(FOLD)], axis=0
        )
        packed = matmul(pick, source).astype(BF16)
        for p in range(peers):
            for g in range(groups):
                first = p * block_rows + g * group_rows
                packed_ref[first : first + group_rows, :] = packed[
                    p * group_rows : (p + 1) * group_rows, g * LANES : (g + 1) * LANES
                ]
            packed_ref[(p + 1) * block_rows - TILE : (p + 1) * block_rows, :] = codes[
                p * TILE : (p + 1) * TILE, :
            ]
        conv_copy.wait()
        stream_of = iota((streams, LANES), 0)
        slot_row = jnp.zeros((streams, LANES), I32)
        for j in range(streams):
            slot_row = jnp.where(stream_of == j, dest_ref[j] % streams + 1, slot_row)
        for c in range(width // LANES):
            conv_f32[c, 0 : tail * streams, :] = conv_ref[:, c * LANES : (c + 1) * LANES].astype(F32)
            conv_f32[c, tail * streams : (tail + 1) * streams, :] = slot_row.astype(F32)
        for out_ref in (up_ref, down_ref):
            out_ref[:, 2 * left : rows, :] = jnp.zeros((MIG, 1 + tail, width), BF16)
        for out_ref, chosen, place, j, slot, copies in moves:

            @pl.when(chosen)
            def _():
                for c in range(width // LANES):
                    out_ref[place, 2 * left : rows, c * LANES : (c + 1) * LANES] = conv_f32[
                        c, pl.ds(j, tail + 1, stride=streams), :
                    ].astype(BF16)
                for copy in copies:
                    copy.wait()

    bundle = pltpu.VMEM((MIG, rows, width), BF16)
    return pl.pallas_call(
        body,
        out_shape=(pltpu.VMEM((peers * block_rows, LANES), BF16), bundle, bundle),
        in_specs=whole(*[pltpu.SMEM] * 2, *[pltpu.VMEM] * 2, *[pl.ANY] * 4),
        out_specs=whole(*[pltpu.VMEM] * 3),
        scratch_shapes=[
            pltpu.VMEM(conv_state.shape, BF16),
            pltpu.VMEM(frames.shape, BF16),
            pltpu.VMEM((width // LANES, (tail + 1) * streams, LANES), F32),
            pltpu.SemaphoreType.DMA((2,)),
            pltpu.SemaphoreType.DMA((2, 2, streams)),
        ],
        compiler_params=pltpu.CompilerParams(vmem_limit_bytes=12 << 20),
        name="pack_all",
    )(
        *map(
            in_hbm,
            (
                destination, own_index(), route_peer.reshape(1, -1), route_pos.reshape(1, -1),
                key_cache, value_cache, conv_state, frames,
            ),
        )
    )


def own_index():
    return lax.axis_index("streams").astype(I32).reshape(1)


def valid_tile(valid_ref, streams, lanes):
    stream_of = iota((streams, lanes), 0)
    valid = jnp.zeros((streams, lanes), I32)
    for s in range(streams):
        valid = jnp.where(stream_of == s, valid_ref[s], valid)
    return valid


def settle_streams(
    from_lower, from_upper, destination, valid_count, key_cache, value_cache, conv_state,
    conv_kernel, span,
):
    streams, left, width = key_cache.shape
    tail = conv_state.shape[0] // streams
    taps = conv_kernel.shape[0]
    groups = width // LANES
    cache = (streams, left, width)
    stored = tail + 1

    def body(
        dest_ref, own_ref, valid_ref, lower_ref, upper_ref, key_hbm, value_hbm, conv_hbm, taps_hbm,
        keys_old, values_old, conv_kept, conv_part, taps_f32,
        key_ref, value_ref, conv_ref, taps_ref, conv_f32, conv_old, sems,
    ):
        copies = [
            pltpu.make_async_copy(source, target, sems.at[n])
            for n, (source, target) in enumerate(
                (
                    (conv_hbm, conv_ref), (key_hbm, key_ref), (value_hbm, value_ref),
                    (taps_hbm, taps_ref),
                )
            )
        ]
        for copy in copies:
            copy.start()
        own = own_ref[0]
        codes = [
            (bundle_ref, j, jnp.max(bundle_ref[j, 2 * left + tail :, :].astype(F32)).astype(I32))
            for bundle_ref in (lower_ref, upper_ref)
            for j in range(MIG)
        ]
        valid = valid_tile(valid_ref, streams, streams * stored)
        column = iota((streams, streams * stored), 1)
        first = iota((streams, streams * stored), 0) * stored + valid
        kept_pick = jnp.concatenate(
            [ones_where((column == first + i) & (valid + i < tail)) for i in range(tail)], axis=0
        )
        for bundle_ref, j, code in codes:

            @pl.when(code > 0)
            def _():
                slot = code - 1
                keys_old[slot] = bundle_ref[j, 0:left, :]
                values_old[slot] = bundle_ref[j, left : 2 * left, :]
                for c in range(groups):
                    conv_old[c, pl.ds(pl.multiple_of(slot * stored, TILE), stored), :] = bundle_ref[
                        j, 2 * left : 2 * left + stored, c * LANES : (c + 1) * LANES
                    ].astype(F32)

        for copy in copies:
            copy.wait()
        for c in range(groups):
            lanes = slice(c * LANES, (c + 1) * LANES)
            taps_f32[c] = taps_ref[:, lanes].astype(F32)
            conv_f32[c, 0 : tail * streams, :] = conv_ref[:, lanes].astype(F32)
            conv_f32[c, tail * streams : stored * streams, :] = jnp.zeros((streams, LANES), F32)
        for j in range(streams):
            target = dest_ref[j]

            @pl.when(target // streams == own)
            def _():
                slot = target % streams
                keys_old[slot] = key_ref[j]
                values_old[slot] = value_ref[j]
                for c in range(groups):
                    conv_old[c, pl.ds(pl.multiple_of(slot * stored, TILE), stored), :] = conv_f32[
                        c, pl.ds(j, stored, stride=streams), :
                    ]

        for c in range(groups):
            lanes = slice(c * LANES, (c + 1) * LANES)
            conv_kept[:, lanes] = matmul(kept_pick, conv_old[c].astype(BF16)).astype(BF16)
            inputs = [conv_old[c, pl.ds(j, streams, stride=stored), :] for j in range(tail)]
            totals = [jnp.zeros((streams, LANES), F32)] * span
            for i in range(taps):
                tap = taps_f32[c, pl.ds(i, streams, stride=0), :]
                for t in range(min(span, tail - i)):
                    totals[t] = totals[t] + tap * inputs[t + i]
            for t in range(span):
                conv_part[c, t * streams : (t + 1) * streams, :] = totals[t]

    return pl.pallas_call(
        body,
        out_shape=(
            pltpu.VMEM(cache, BF16),
            pltpu.VMEM(cache, BF16),
            pltpu.VMEM((tail * streams, width), BF16),
            pltpu.VMEM((groups, span * streams, LANES), F32),
            pltpu.VMEM((groups, taps, LANES), F32),
        ),
        in_specs=whole(*[pltpu.SMEM] * 3, *[pltpu.VMEM] * 2, *[pl.ANY] * 4),
        out_specs=whole(*[pltpu.VMEM] * 5),
        scratch_shapes=[
            pltpu.VMEM(cache, BF16),
            pltpu.VMEM(cache, BF16),
            pltpu.VMEM(conv_state.shape, BF16),
            pltpu.VMEM(conv_kernel.shape, BF16),
            pltpu.VMEM((groups, stored * streams, LANES), F32),
            pltpu.VMEM((groups, stored * streams, LANES), F32),
            pltpu.SemaphoreType.DMA((4,)),
        ],
        compiler_params=pltpu.CompilerParams(vmem_limit_bytes=16 << 20),
        name="settle_streams",
    )(
        *map(in_hbm, (destination, own_index(), valid_count)),
        in_vmem(from_lower), in_vmem(from_upper),
        *map(in_hbm, (key_cache, value_cache, conv_state, conv_kernel)),
    )


def stream_step(received, valid_count, settled, qkv_weight, peers, row_count, capacity):
    keys_settled, _, conv_settled, _, taps_settled = settled
    streams, left, width = keys_settled.shape
    tail = conv_settled.shape[0] // streams
    taps = taps_settled.shape[1]
    span = row_count // streams
    model, columns = qkv_weight.shape
    half = model // FOLD
    heads = width // HEAD
    keys = left + span
    lane_groups = width // LANES
    edges = [columns * n // SPLIT for n in CHUNK_EDGES]
    slots, group_rows, groups, block_rows = block_sizes(model, capacity)
    packed_rows = peers * group_rows

    def body(
        valid_ref, recv_ref, keys_old, values_old, conv_kept, conv_part, taps_f32, weight_hbm,
        encoded_hbm, keys_next_hbm, values_next_hbm, conv_next_hbm,
        encoded_ref, keys_next_ref, values_next_ref, conv_next_ref,
        weight_ref, gathered, qkv_ref, attended_ref, attended_f32, encoded_f32,
        weight_sems, out_sems,
    ):
        weight_copies = [
            pltpu.make_async_copy(
                weight_hbm.at[:, first:last], weight_ref.at[:, first:last], weight_sems.at[n]
            )
            for n, (first, last) in enumerate(zip(edges, edges[1:]))
        ]
        out_copies = [
            pltpu.make_async_copy(source, target, out_sems.at[n])
            for n, (source, target) in enumerate(
                (
                    (encoded_ref, encoded_hbm), (keys_next_ref, keys_next_hbm),
                    (values_next_ref, values_next_hbm), (conv_next_ref, conv_next_hbm),
                )
            )
        ]
        for copy in weight_copies[:AHEAD]:
            copy.start()

        for p in range(peers):
            for g in range(groups):
                gathered[p * group_rows : (p + 1) * group_rows, g * LANES : (g + 1) * LANES] = recv_ref[
                    p * block_rows + g * group_rows : p * block_rows + (g + 1) * group_rows, :
                ]
        codes = jnp.concatenate(
            [recv_ref[(p + 1) * block_rows - TILE : (p + 1) * block_rows, :] for p in range(peers)],
            axis=0,
        )
        spread_lane = ones_where(
            iota((LANES, packed_rows), 1) % group_rows == iota((LANES, packed_rows), 0)
        )
        spread = matmul(codes, spread_lane)
        column = iota((peers * TILE, packed_rows), 1)
        own_tile = iota((peers * TILE, packed_rows), 0) == column // group_rows * TILE
        position = jnp.sum(jnp.where(own_tile, spread, 0.0), axis=0, keepdims=True).astype(I32)
        out_row = iota((row_count, packed_rows), 0) + 1
        column_half = iota((row_count, packed_rows), 1) % group_rows // slots
        hit = out_row == position
        place = jnp.concatenate([ones_where(hit & (column_half == h)) for h in range(FOLD)], axis=0)
        halves = matmul(place, gathered[...])
        owned = jnp.concatenate(
            [halves[h * row_count : (h + 1) * row_count, :] for h in range(FOLD)], axis=1
        )
        centered = owned - jnp.mean(owned, axis=-1, keepdims=True)
        spread_of = jnp.mean(centered * centered, axis=-1, keepdims=True)
        normed = (centered * lax.rsqrt(spread_of + EPSILON)).astype(BF16)
        for n, (first, last) in enumerate(zip(edges, edges[1:])):
            weight_copies[n].wait()
            for copy in weight_copies[n + AHEAD : n + AHEAD + 1]:
                copy.start()
            qkv_ref[:, first:last] = matmul(normed, weight_ref[:, first:last]).astype(BF16)

        head_rows = heads * span
        head_mask = ones_where(
            iota((head_rows, width), 1) // HEAD == iota((head_rows, width), 0) // span
        )
        t_of = iota((keys, head_rows), 1) % span
        key_of = iota((keys, head_rows), 0) - left
        causal = key_of <= t_of
        t_row = iota((span, LANES), 0)
        lane = iota((span, LANES), 1)
        all_rows = [slice(s * span, (s + 1) * span) for s in range(streams)]
        all_keys = [
            jnp.concatenate([keys_old[s], qkv_ref[all_rows[s], width : 2 * width]], axis=0)
            for s in range(streams)
        ]
        all_values = [
            jnp.concatenate([values_old[s], qkv_ref[all_rows[s], 2 * width : 3 * width]], axis=0)
            for s in range(streams)
        ]
        all_scores = []
        for first in range(0, streams, 2):
            pair = range(first, first + 2)
            queries = [
                jnp.concatenate([qkv_ref[all_rows[s], 0:width]] * heads, axis=0) * head_mask
                for s in pair
            ]
            scores = matmul_nt(
                jnp.concatenate([all_keys[s] for s in pair], axis=0),
                jnp.concatenate(queries, axis=0),
            )
            all_scores += [
                scores[n * keys : (n + 1) * keys, n * head_rows : (n + 1) * head_rows]
                for n in range(2)
            ]
        all_probabilities = []
        for s in range(streams):
            allowed = (key_of < 0) | (causal & (key_of < valid_ref[s]))
            scores = jnp.where(allowed, all_scores[s] * HEAD ** (-0.5), -1e30)
            weights = jnp.exp(scores - jnp.max(scores, axis=0, keepdims=True))
            all_probabilities.append(
                (weights / jnp.sum(weights, axis=0, keepdims=True)).astype(BF16)
            )
        shift = iota((left, GROUP * keys), 1) - iota((left, GROUP * keys), 0)
        for first in range(0, streams, GROUP):
            group = range(first, first + GROUP)
            pick = jnp.concatenate(
                [ones_where(shift == valid_ref[s] + (s - first) * keys) for s in group], axis=0
            )
            for source, target in ((all_keys, keys_next_ref), (all_values, values_next_ref)):
                target[first * left : (first + GROUP) * left, :] = matmul(
                    pick, jnp.concatenate([source[s] for s in group], axis=0)
                ).astype(BF16)
        out_copies[1].start()
        out_copies[2].start()
        all_mixed = [
            lax.dot_general(
                all_probabilities[s], all_values[s], (((0,), (0,)), ((), ())),
                preferred_element_type=F32,
            )
            for s in range(streams)
        ]
        for s in range(streams):
            for c in range(lane_groups):
                lanes = slice(c * LANES, (c + 1) * LANES)
                first = c * LANES // HEAD
                last = ((c + 1) * LANES - 1) // HEAD
                attended = all_mixed[s][first * span : (first + 1) * span, lanes]
                for h in range(first + 1, last + 1):
                    attended = jnp.where(
                        lane >= h * HEAD - c * LANES,
                        all_mixed[s][h * span : (h + 1) * span, lanes],
                        attended,
                    )
                attended = jnp.where(t_row < valid_ref[s], attended, 0.0).astype(BF16)
                attended_ref[all_rows[s], lanes] = attended
                attended_f32[c, all_rows[s], :] = attended.astype(F32)

        valid = valid_tile(valid_ref, streams, row_count)
        column = iota((streams, row_count), 1)
        frame = valid - tail
        first = iota((streams, row_count), 0) * span + frame
        new_pick = jnp.concatenate(
            [ones_where((column == first + i) & (frame + i >= 0)) for i in range(tail)], axis=0
        )
        conv_next_ref[...] = conv_kept[...] + matmul(new_pick, attended_ref[...]).astype(BF16)
        out_copies[3].start()

        valid = valid_tile(valid_ref, streams, LANES)
        for c in range(lane_groups):
            inputs = [attended_f32[c, pl.ds(t, streams, stride=span), :] for t in range(span)]
            totals = [
                conv_part[c, t * streams : (t + 1) * streams, :] + inputs[t] for t in range(span)
            ]
            for i in range(max(tail - span + 1, 0), taps):
                tap = taps_f32[c, pl.ds(i, streams, stride=0), :]
                for t in range(max(tail - i, 0), min(span, span + tail - i)):
                    totals[t] = totals[t] + tap * inputs[t + i - tail]
            for t in range(span):
                encoded_f32[c, pl.ds(t, streams, stride=span), :] = jnp.where(
                    t < valid, totals[t], 0.0
                )
        for c in range(lane_groups):
            encoded_ref[:, c * LANES : (c + 1) * LANES] = encoded_f32[c].astype(BF16)
        out_copies[0].start()
        for copy in out_copies:
            copy.wait()

    cache = (streams * left, width)
    by_lane_group = pltpu.VMEM((lane_groups, row_count, LANES), F32)
    out_shapes = ((row_count, width), cache, cache, (tail * streams, width))
    return pl.pallas_call(
        body,
        out_shape=[jax.ShapeDtypeStruct(shape, BF16) for shape in out_shapes],
        in_specs=whole(pltpu.SMEM, *[pltpu.VMEM] * 6, pl.ANY),
        out_specs=whole(*[pl.ANY] * 4),
        scratch_shapes=[
            *[pltpu.VMEM(shape, BF16) for shape in out_shapes],
            pltpu.VMEM((model, columns), BF16),
            pltpu.VMEM((packed_rows, half), BF16),
            pltpu.VMEM((row_count, columns), BF16),
            pltpu.VMEM((row_count, width), BF16),
            by_lane_group,
            by_lane_group,
            pltpu.SemaphoreType.DMA((len(edges) - 1,)),
            pltpu.SemaphoreType.DMA((4,)),
        ],
        compiler_params=pltpu.CompilerParams(vmem_limit_bytes=32 << 20),
        name="stream_step",
    )(
        in_hbm(valid_count), in_vmem(received), *map(in_vmem, settled), in_hbm(qkv_weight)
    )


def from_behind(block, axis, distance):
    count = lax.axis_size(axis)
    return lax.ppermute(block, axis, [((i - distance) % count, i) for i in range(count)])


def local(
    frames, route_peer, route_pos, destination, valid_count, key_cache, value_cache, conv_state,
    qkv_weight, conv_kernel,
):
    peers = lax.axis_size("streams")
    row_count = frames.shape[0]
    per_peer = row_count // peers
    capacity = per_peer + per_peer // 2
    streams, left, width = key_cache.shape
    conv_by_time = conv_state.transpose(1, 0, 2).reshape(-1, width)
    packed, up, down = pack_all(
        frames, route_peer, route_pos, destination, key_cache, value_cache, conv_by_time,
        peers, capacity,
    )
    from_lower = from_behind(up, "streams", 1)
    from_upper = from_behind(down, "streams", -1)
    received = lax.all_to_all(packed, "streams", split_axis=0, concat_axis=0, tiled=True)
    settled = settle_streams(
        from_lower, from_upper, destination, valid_count, key_cache, value_cache,
        conv_by_time, conv_kernel, row_count // streams,
    )
    encoded, keys_next, values_next, conv_next = stream_step(
        received, valid_count, settled, qkv_weight, peers, row_count, capacity
    )
    cache = (streams, left, width)
    return (
        encoded, keys_next.reshape(cache), values_next.reshape(cache),
        conv_next.reshape(-1, streams, width).transpose(1, 0, 2),
    )


def solution(mesh):
    rows = P(("groups", "streams"))
    return jax.shard_map(
        local,
        mesh=mesh,
        in_specs=(rows,) * 8 + (P(), P()),
        out_specs=(rows,) * 4,
        check_vma=False,
    )
```

```python
import jax
import jax.numpy as jnp
from jax import lax
from jax.experimental import pallas as pl
from jax.experimental.pallas import tpu as pltpu
from jax.sharding import PartitionSpec as P


HEAD = 96
MIG = 4
EPSILON = 1e-05
LANES = 128
TILE = 8
FOLD = 2
GROUP = 4
SPLIT = 9
CHUNK_EDGES = (0, 3, 6, 9)
VALUES_FROM = 2
PIECE = 6

BF16 = jnp.bfloat16
F32 = jnp.float32
I32 = jnp.int32


def iota(shape, axis):
    return lax.broadcasted_iota(I32, shape, axis)


def ones_where(condition):
    return jnp.where(condition, 1.0, 0.0).astype(BF16)


def matmul(left, right):
    return jnp.dot(left, right, preferred_element_type=F32)


def matmul_nt(left, right):
    return lax.dot_general(left, right, (((1,), (1,)), ((), ())), preferred_element_type=F32)


def in_vmem(array):
    return pltpu.with_memory_space_constraint(array, pltpu.VMEM)


def in_hbm(array):
    return pltpu.with_memory_space_constraint(array, pltpu.HBM)


def start_copies(pairs, sems):
    copies = [
        pltpu.make_async_copy(source, target, sems.at[n])
        for n, (source, target) in enumerate(pairs)
    ]
    for copy in copies:
        copy.start()
    return copies


def round_up(value, multiple):
    return -(-value // multiple) * multiple


def whole(*spaces):
    return [pl.BlockSpec(memory_space=space) for space in spaces]


def block_sizes(width, capacity):
    slots = round_up(capacity, TILE // FOLD)
    group_rows = FOLD * slots
    groups = width // FOLD // LANES
    return slots, group_rows, groups, groups * group_rows + TILE


def pack_all(
    frames, route_peer, route_pos, destination, key_cache, value_cache, conv_state, peers, capacity
):
    row_count, model = frames.shape
    slots, group_rows, groups, block_rows = block_sizes(model, capacity)
    half = model // FOLD
    streams, left, width = key_cache.shape
    tail = conv_state.shape[0] // streams
    rows = 2 * left + tail + 1

    def body(
        dest_hbm, own_hbm, peer_hbm, pos_hbm, key_hbm, value_hbm, conv_hbm, frames_hbm,
        packed_hbm, up_ref, down_ref, packed_ref, conv_ref, frames_ref, conv_f32, dest_ref, own_ref,
        peer_ref, pos_ref, sems, small_sems, move_sems,
    ):
        frames_copy = pltpu.make_async_copy(frames_hbm, frames_ref, sems.at[0])
        conv_copy = pltpu.make_async_copy(conv_hbm, conv_ref, sems.at[1])
        small_copies = start_copies(
            ((peer_hbm, peer_ref), (pos_hbm, pos_ref), (dest_hbm, dest_ref), (own_hbm, own_ref)),
            small_sems,
        )
        frames_copy.start()
        conv_copy.start()
        for copy in small_copies:
            copy.wait()
        own = own_ref[0]
        moves = []
        for n, (out_ref, device) in enumerate(
            ((up_ref, (own + 1) % peers), (down_ref, (own + peers - 1) % peers))
        ):
            rank = jnp.int32(0)
            for j in range(streams):
                target = dest_ref[j]
                chosen = target // streams == device
                place = jnp.minimum(rank, MIG - 1)
                copies = [
                    pltpu.make_async_copy(
                        source.at[j],
                        out_ref.at[place, k * left : (k + 1) * left, :],
                        move_sems.at[n, k, j],
                    )
                    for k, source in enumerate((key_hbm, value_hbm))
                ]

                @pl.when(chosen)
                def _():
                    for copy in copies:
                        copy.start()

                moves.append((out_ref, chosen, place, j, target % streams, copies))
                rank = rank + chosen.astype(I32)

        peer = peer_ref[...]
        owner = ones_where(iota((peers, row_count), 0) == peer)
        earlier = ones_where(iota((row_count, row_count), 0) < iota((row_count, row_count), 1))
        running = matmul(owner, earlier)
        slot = jnp.sum(running * owner.astype(F32), axis=0, keepdims=True).astype(I32)
        flat = peer * group_rows + slot
        packed_row = iota((peers * group_rows, row_count), 0)
        pick = jnp.concatenate(
            [ones_where(packed_row == flat + h * slots) for h in range(FOLD)], axis=1
        )
        owner_tile = ones_where(iota((peers * TILE, row_count), 0) // TILE == peer)
        lane = iota((LANES, row_count), 0)
        in_lane = (lane % slots == slot) & (lane < group_rows)
        code = jnp.where(in_lane, (pos_ref[...] + 1).astype(F32), 0.0).astype(BF16)
        codes = matmul_nt(owner_tile, code).astype(BF16)
        frames_copy.wait()
        source = jnp.concatenate(
            [frames_ref[:, h * half : (h + 1) * half] for h in range(FOLD)], axis=0
        )
        packed = matmul(pick, source).astype(BF16)
        for p in range(peers):
            for g in range(groups):
                first = p * block_rows + g * group_rows
                packed_ref[first : first + group_rows, :] = packed[
                    p * group_rows : (p + 1) * group_rows, g * LANES : (g + 1) * LANES
                ]
            packed_ref[(p + 1) * block_rows - TILE : (p + 1) * block_rows, :] = codes[
                p * TILE : (p + 1) * TILE, :
            ]
        packed_copy = pltpu.make_async_copy(packed_ref, packed_hbm, sems.at[2])
        packed_copy.start()
        conv_copy.wait()
        stream_of = iota((streams, LANES), 0)
        slot_row = jnp.zeros((streams, LANES), I32)
        for j in range(streams):
            slot_row = jnp.where(stream_of == j, dest_ref[j] % streams + 1, slot_row)
        for c in range(width // LANES):
            conv_f32[c, 0 : tail * streams, :] = conv_ref[:, c * LANES : (c + 1) * LANES].astype(F32)
            conv_f32[c, tail * streams : (tail + 1) * streams, :] = slot_row.astype(F32)
        for out_ref in (up_ref, down_ref):
            out_ref[:, 2 * left : rows, :] = jnp.zeros((MIG, 1 + tail, width), BF16)
        for out_ref, chosen, place, j, slot, copies in moves:

            @pl.when(chosen)
            def _():
                for c in range(width // LANES):
                    out_ref[place, 2 * left : rows, c * LANES : (c + 1) * LANES] = conv_f32[
                        c, pl.ds(j, tail + 1, stride=streams), :
                    ].astype(BF16)
                for copy in copies:
                    copy.wait()

        packed_copy.wait()

    packed_shape = (peers * block_rows, LANES)
    bundle = pltpu.VMEM((MIG, rows, width), BF16)
    return pl.pallas_call(
        body,
        out_shape=(pltpu.HBM(packed_shape, BF16), bundle, bundle),
        in_specs=whole(*[pl.ANY] * 8),
        out_specs=whole(pl.ANY, pltpu.VMEM, pltpu.VMEM),
        scratch_shapes=[
            pltpu.VMEM(packed_shape, BF16),
            pltpu.VMEM(conv_state.shape, BF16),
            pltpu.VMEM(frames.shape, BF16),
            pltpu.VMEM((width // LANES, (tail + 1) * streams, LANES), F32),
            pltpu.SMEM((streams,), I32),
            pltpu.SMEM((1,), I32),
            pltpu.VMEM((1, row_count), I32),
            pltpu.VMEM((1, row_count), I32),
            pltpu.SemaphoreType.DMA((3,)),
            pltpu.SemaphoreType.DMA((4,)),
            pltpu.SemaphoreType.DMA((2, 2, streams)),
        ],
        compiler_params=pltpu.CompilerParams(vmem_limit_bytes=12 << 20),
        name="pack_all",
    )(
        *map(
            in_hbm,
            (
                destination, own_index(), route_peer.reshape(1, -1), route_pos.reshape(1, -1),
                key_cache, value_cache, conv_state, frames,
            ),
        )
    )


def own_index():
    return lax.axis_index("streams").astype(I32).reshape(1)


def valid_tile(valid_ref, streams, lanes):
    stream_of = iota((streams, lanes), 0)
    valid = jnp.zeros((streams, lanes), I32)
    for s in range(streams):
        valid = jnp.where(stream_of == s, valid_ref[s], valid)
    return valid


def settle_streams(
    from_lower, from_upper, destination, valid_count, key_cache, value_cache, conv_state,
    conv_kernel, span,
):
    streams, left, width = key_cache.shape
    tail = conv_state.shape[0] // streams
    taps = conv_kernel.shape[0]
    groups = width // LANES
    cache = (streams, left, width)
    stored = tail + 1

    def body(
        dest_hbm, own_hbm, valid_hbm, lower_ref, upper_ref, key_hbm, value_hbm, conv_hbm, taps_hbm,
        keys_old, values_old, conv_kept, conv_part, taps_f32,
        key_ref, value_ref, conv_ref, taps_ref, conv_f32, conv_old, dest_ref, own_ref, valid_ref,
        sems, small_sems,
    ):
        small_copies = start_copies(
            ((dest_hbm, dest_ref), (own_hbm, own_ref), (valid_hbm, valid_ref)), small_sems
        )
        copies = start_copies(
            (
                (conv_hbm, conv_ref), (key_hbm, key_ref), (value_hbm, value_ref),
                (taps_hbm, taps_ref),
            ),
            sems,
        )
        codes = [
            (bundle_ref, j, jnp.max(bundle_ref[j, 2 * left + tail :, :].astype(F32)).astype(I32))
            for bundle_ref in (lower_ref, upper_ref)
            for j in range(MIG)
        ]
        for copy in small_copies:
            copy.wait()
        own = own_ref[0]
        valid = valid_tile(valid_ref, streams, streams * stored)
        column = iota((streams, streams * stored), 1)
        first = iota((streams, streams * stored), 0) * stored + valid
        kept_pick = jnp.concatenate(
            [ones_where((column == first + i) & (valid + i < tail)) for i in range(tail)], axis=0
        )
        for bundle_ref, j, code in codes:

            @pl.when(code > 0)
            def _():
                slot = code - 1
                keys_old[slot] = bundle_ref[j, 0:left, :]
                values_old[slot] = bundle_ref[j, left : 2 * left, :]
                for c in range(groups):
                    conv_old[c, pl.ds(pl.multiple_of(slot * stored, TILE), stored), :] = bundle_ref[
                        j, 2 * left : 2 * left + stored, c * LANES : (c + 1) * LANES
                    ].astype(F32)

        for copy in copies:
            copy.wait()
        for c in range(groups):
            lanes = slice(c * LANES, (c + 1) * LANES)
            taps_f32[c] = taps_ref[:, lanes].astype(F32)
            conv_f32[c, 0 : tail * streams, :] = conv_ref[:, lanes].astype(F32)
            conv_f32[c, tail * streams : stored * streams, :] = jnp.zeros((streams, LANES), F32)
        for j in range(streams):
            target = dest_ref[j]

            @pl.when(target // streams == own)
            def _():
                slot = target % streams
                keys_old[slot] = key_ref[j]
                values_old[slot] = value_ref[j]
                for c in range(groups):
                    conv_old[c, pl.ds(pl.multiple_of(slot * stored, TILE), stored), :] = conv_f32[
                        c, pl.ds(j, stored, stride=streams), :
                    ]

        for c in range(groups):
            lanes = slice(c * LANES, (c + 1) * LANES)
            conv_kept[:, lanes] = matmul(kept_pick, conv_old[c].astype(BF16)).astype(BF16)
            inputs = [conv_old[c, pl.ds(j, streams, stride=stored), :] for j in range(tail)]
            totals = [jnp.zeros((streams, LANES), F32)] * span
            for i in range(taps):
                tap = taps_f32[c, pl.ds(i, streams, stride=0), :]
                for t in range(min(span, tail - i)):
                    totals[t] = totals[t] + tap * inputs[t + i]
            for t in range(span):
                conv_part[c, t * streams : (t + 1) * streams, :] = totals[t]

    return pl.pallas_call(
        body,
        out_shape=(
            pltpu.VMEM(cache, BF16),
            pltpu.VMEM(cache, BF16),
            pltpu.VMEM((tail * streams, width), BF16),
            pltpu.VMEM((groups, span * streams, LANES), F32),
            pltpu.VMEM((groups, taps, LANES), F32),
        ),
        in_specs=whole(*[pl.ANY] * 3, *[pltpu.VMEM] * 2, *[pl.ANY] * 4),
        out_specs=whole(*[pltpu.VMEM] * 5),
        scratch_shapes=[
            pltpu.VMEM(cache, BF16),
            pltpu.VMEM(cache, BF16),
            pltpu.VMEM(conv_state.shape, BF16),
            pltpu.VMEM(conv_kernel.shape, BF16),
            pltpu.VMEM((groups, stored * streams, LANES), F32),
            pltpu.VMEM((groups, stored * streams, LANES), F32),
            pltpu.SMEM((streams,), I32),
            pltpu.SMEM((1,), I32),
            pltpu.SMEM((streams,), I32),
            pltpu.SemaphoreType.DMA((4,)),
            pltpu.SemaphoreType.DMA((3,)),
        ],
        compiler_params=pltpu.CompilerParams(vmem_limit_bytes=16 << 20),
        name="settle_streams",
    )(
        *map(in_hbm, (destination, own_index(), valid_count)),
        in_vmem(from_lower), in_vmem(from_upper),
        *map(in_hbm, (key_cache, value_cache, conv_state, conv_kernel)),
    )


def stream_step(received, valid_count, settled, qkv_weight, peers, row_count, capacity):
    keys_settled, _, conv_settled, _, taps_settled = settled
    streams, left, width = keys_settled.shape
    tail = conv_settled.shape[0] // streams
    taps = taps_settled.shape[1]
    span = row_count // streams
    model, columns = qkv_weight.shape
    half = model // FOLD
    heads = width // HEAD
    keys = left + span
    lane_groups = width // LANES
    edges = [columns * n // SPLIT for n in CHUNK_EDGES]
    slots, group_rows, groups, block_rows = block_sizes(model, capacity)
    packed_rows = peers * group_rows

    def body(
        valid_hbm, recv_ref, keys_old, values_old, conv_kept, conv_part, taps_f32, weight_hbm,
        encoded_hbm, keys_next_hbm, values_next_hbm, conv_next_hbm,
        encoded_ref, keys_next_ref, values_next_ref, conv_next_ref,
        weight_ref, gathered, qkv_ref, attended_ref, attended_f32, encoded_f32, valid_ref,
        weight_sems, out_sems, valid_sem,
    ):
        weight_copies = [
            pltpu.make_async_copy(
                weight_hbm.at[:, first:last], weight_ref.at[:, first:last], weight_sems.at[n]
            )
            for n, (first, last) in enumerate(zip(edges, edges[1:]))
        ]
        for copy in weight_copies:
            copy.start()
        valid_copy = pltpu.make_async_copy(valid_hbm, valid_ref, valid_sem)
        valid_copy.start()

        for p in range(peers):
            for g in range(groups):
                gathered[p * group_rows : (p + 1) * group_rows, g * LANES : (g + 1) * LANES] = recv_ref[
                    p * block_rows + g * group_rows : p * block_rows + (g + 1) * group_rows, :
                ]
        codes = jnp.concatenate(
            [recv_ref[(p + 1) * block_rows - TILE : (p + 1) * block_rows, :] for p in range(peers)],
            axis=0,
        )
        spread_lane = ones_where(
            iota((LANES, packed_rows), 1) % group_rows == iota((LANES, packed_rows), 0)
        )
        spread = matmul(codes, spread_lane)
        column = iota((peers * TILE, packed_rows), 1)
        own_tile = iota((peers * TILE, packed_rows), 0) == column // group_rows * TILE
        position = jnp.sum(jnp.where(own_tile, spread, 0.0), axis=0, keepdims=True).astype(I32)
        out_row = iota((row_count, packed_rows), 0) + 1
        column_half = iota((row_count, packed_rows), 1) % group_rows // slots
        hit = out_row == position
        place = jnp.concatenate([ones_where(hit & (column_half == h)) for h in range(FOLD)], axis=0)
        halves = matmul(place, gathered[...])
        owned = jnp.concatenate(
            [halves[h * row_count : (h + 1) * row_count, :] for h in range(FOLD)], axis=1
        )
        centered = owned - jnp.mean(owned, axis=-1, keepdims=True)
        spread_of = jnp.mean(centered * centered, axis=-1, keepdims=True)
        normed = (centered * lax.rsqrt(spread_of + EPSILON)).astype(BF16)

        def project(n):
            weight_copies[n].wait()
            columns_of = slice(edges[n], edges[n + 1])
            qkv_ref[:, columns_of] = matmul(normed, weight_ref[:, columns_of]).astype(BF16)

        for n in range(VALUES_FROM):
            project(n)
        valid_copy.wait()

        head_rows = heads * span
        head_mask = ones_where(
            iota((head_rows, width), 1) // HEAD == iota((head_rows, width), 0) // span
        )
        t_of = iota((keys, head_rows), 1) % span
        key_of = iota((keys, head_rows), 0) - left
        causal = key_of <= t_of
        t_row = iota((span, LANES), 0)
        lane = iota((span, LANES), 1)
        all_rows = [slice(s * span, (s + 1) * span) for s in range(streams)]
        all_keys = [
            jnp.concatenate([keys_old[s], qkv_ref[all_rows[s], width : 2 * width]], axis=0)
            for s in range(streams)
        ]
        all_scores = []
        for first in range(0, streams, 2):
            pair = range(first, first + 2)
            queries = [
                jnp.concatenate([qkv_ref[all_rows[s], 0:width]] * heads, axis=0) * head_mask
                for s in pair
            ]
            scores = matmul_nt(
                jnp.concatenate([all_keys[s] for s in pair], axis=0),
                jnp.concatenate(queries, axis=0),
            )
            all_scores += [
                scores[n * keys : (n + 1) * keys, n * head_rows : (n + 1) * head_rows]
                for n in range(2)
            ]
        all_probabilities = []
        for s in range(streams):
            allowed = (key_of < 0) | (causal & (key_of < valid_ref[s]))
            scores = jnp.where(allowed, all_scores[s] * HEAD ** (-0.5), -1e30)
            weights = jnp.exp(scores - jnp.max(scores, axis=0, keepdims=True))
            all_probabilities.append(
                (weights / jnp.sum(weights, axis=0, keepdims=True)).astype(BF16)
            )
        shift = iota((left, GROUP * keys), 1) - iota((left, GROUP * keys), 0)
        groups_of = [range(first, first + GROUP) for first in range(0, streams, GROUP)]
        picks = [
            jnp.concatenate(
                [ones_where(shift == valid_ref[s] + n * keys) for n, s in enumerate(group)], axis=0
            )
            for group in groups_of
        ]

        def shifted(source, target):
            for group, pick in zip(groups_of, picks):
                target[group[0] * left : (group[-1] + 1) * left, :] = matmul(
                    pick, jnp.concatenate([source[s] for s in group], axis=0)
                ).astype(BF16)

        shifted(all_keys, keys_next_ref)
        keys_copy = pltpu.make_async_copy(keys_next_ref, keys_next_hbm, out_sems.at[0])
        keys_copy.start()
        out_copies = [keys_copy]
        valid = valid_tile(valid_ref, streams, row_count)
        column = iota((streams, row_count), 1)
        frame = valid - tail
        first = iota((streams, row_count), 0) * span + frame
        new_pick = jnp.concatenate(
            [ones_where((column == first + i) & (frame + i >= 0)) for i in range(tail)], axis=0
        )
        valid = valid_tile(valid_ref, streams, LANES)

        for piece in range(lane_groups // PIECE):
            project(VALUES_FROM + piece)
            lanes = slice(piece * PIECE * LANES, (piece + 1) * PIECE * LANES)
            all_values = [
                jnp.concatenate(
                    [
                        values_old[s, :, lanes],
                        qkv_ref[all_rows[s], 2 * width + lanes.start : 2 * width + lanes.stop],
                    ],
                    axis=0,
                )
                for s in range(streams)
            ]
            all_mixed = [
                lax.dot_general(
                    all_probabilities[s], all_values[s], (((0,), (0,)), ((), ())),
                    preferred_element_type=F32,
                )
                for s in range(streams)
            ]
            for group, pick in zip(groups_of, picks):
                values_next_ref[group[0] * left : (group[-1] + 1) * left, lanes] = matmul(
                    pick, jnp.concatenate([all_values[s] for s in group], axis=0)
                ).astype(BF16)
            for s in range(streams):
                for n in range(PIECE):
                    c = piece * PIECE + n
                    here = slice(n * LANES, (n + 1) * LANES)
                    first = c * LANES // HEAD
                    last = ((c + 1) * LANES - 1) // HEAD
                    attended = all_mixed[s][first * span : (first + 1) * span, here]
                    for h in range(first + 1, last + 1):
                        attended = jnp.where(
                            lane >= h * HEAD - c * LANES,
                            all_mixed[s][h * span : (h + 1) * span, here],
                            attended,
                        )
                    attended = jnp.where(t_row < valid_ref[s], attended, 0.0).astype(BF16)
                    attended_ref[all_rows[s], c * LANES : (c + 1) * LANES] = attended
                    attended_f32[c, all_rows[s], :] = attended.astype(F32)
            conv_next_ref[:, lanes] = conv_kept[:, lanes] + matmul(
                new_pick, attended_ref[:, lanes]
            ).astype(BF16)
            for c in range(piece * PIECE, (piece + 1) * PIECE):
                inputs = [attended_f32[c, pl.ds(t, streams, stride=span), :] for t in range(span)]
                totals = [
                    conv_part[c, t * streams : (t + 1) * streams, :] + inputs[t]
                    for t in range(span)
                ]
                for i in range(max(tail - span + 1, 0), taps):
                    tap = taps_f32[c, pl.ds(i, streams, stride=0), :]
                    for t in range(max(tail - i, 0), min(span, span + tail - i)):
                        totals[t] = totals[t] + tap * inputs[t + i - tail]
                for t in range(span):
                    encoded_f32[c, pl.ds(t, streams, stride=span), :] = jnp.where(
                        t < valid, totals[t], 0.0
                    )
                encoded_ref[:, c * LANES : (c + 1) * LANES] = encoded_f32[c].astype(BF16)
            for n, (source, target) in enumerate(
                (
                    (values_next_ref, values_next_hbm), (conv_next_ref, conv_next_hbm),
                    (encoded_ref, encoded_hbm),
                )
            ):
                copy = pltpu.make_async_copy(
                    source.at[:, lanes], target.at[:, lanes], out_sems.at[1 + 3 * piece + n]
                )
                copy.start()
                out_copies.append(copy)
        for copy in out_copies:
            copy.wait()

    cache = (streams * left, width)
    by_lane_group = pltpu.VMEM((lane_groups, row_count, LANES), F32)
    out_shapes = ((row_count, width), cache, cache, (tail * streams, width))
    return pl.pallas_call(
        body,
        out_shape=[jax.ShapeDtypeStruct(shape, BF16) for shape in out_shapes],
        in_specs=whole(pl.ANY, *[pltpu.VMEM] * 6, pl.ANY),
        out_specs=whole(*[pl.ANY] * 4),
        scratch_shapes=[
            *[pltpu.VMEM(shape, BF16) for shape in out_shapes],
            pltpu.VMEM((model, columns), BF16),
            pltpu.VMEM((packed_rows, half), BF16),
            pltpu.VMEM((row_count, columns), BF16),
            pltpu.VMEM((row_count, width), BF16),
            by_lane_group,
            by_lane_group,
            pltpu.SMEM((streams,), I32),
            pltpu.SemaphoreType.DMA((len(edges) - 1,)),
            pltpu.SemaphoreType.DMA((1 + 3 * (lane_groups // PIECE),)),
            pltpu.SemaphoreType.DMA,
        ],
        compiler_params=pltpu.CompilerParams(vmem_limit_bytes=32 << 20),
        name="stream_step",
    )(
        in_hbm(valid_count), in_vmem(received), *map(in_vmem, settled), in_hbm(qkv_weight)
    )


def from_behind(block, axis, distance):
    count = lax.axis_size(axis)
    return lax.ppermute(block, axis, [((i - distance) % count, i) for i in range(count)])


def local(
    frames, route_peer, route_pos, destination, valid_count, key_cache, value_cache, conv_state,
    qkv_weight, conv_kernel,
):
    peers = lax.axis_size("streams")
    row_count = frames.shape[0]
    per_peer = row_count // peers
    capacity = per_peer + per_peer // 2
    streams, left, width = key_cache.shape
    conv_by_time = conv_state.transpose(1, 0, 2).reshape(-1, width)
    packed, up, down = pack_all(
        frames, route_peer, route_pos, destination, key_cache, value_cache, conv_by_time,
        peers, capacity,
    )
    from_lower = from_behind(up, "streams", 1)
    from_upper = from_behind(down, "streams", -1)
    received = lax.all_to_all(packed, "streams", split_axis=0, concat_axis=0, tiled=True)
    settled = settle_streams(
        from_lower, from_upper, destination, valid_count, key_cache, value_cache,
        conv_by_time, conv_kernel, row_count // streams,
    )
    encoded, keys_next, values_next, conv_next = stream_step(
        received, valid_count, settled, qkv_weight, peers, row_count, capacity
    )
    cache = (streams, left, width)
    return (
        encoded, keys_next.reshape(cache), values_next.reshape(cache),
        conv_next.reshape(-1, streams, width).transpose(1, 0, 2),
    )


def solution(mesh):
    rows = P(("groups", "streams"))
    return jax.shard_map(
        local,
        mesh=mesh,
        in_specs=(rows,) * 8 + (P(), P()),
        out_specs=(rows,) * 4,
        check_vma=False,
    )
```

```python
import jax
import jax.numpy as jnp
from jax import lax
from jax.experimental import pallas as pl
from jax.experimental.pallas import tpu as pltpu
from jax.sharding import PartitionSpec as P


HEAD = 96
MIG = 4
EPSILON = 1e-05
LANES = 128
TILE = 8
FOLD = 2
GROUP = 4
SPLIT = 9
CHUNK_EDGES = (0, 3, 6, 9)
VALUES_FROM = 2
PIECE = 6

BF16 = jnp.bfloat16
F32 = jnp.float32
I32 = jnp.int32


def iota(shape, axis):
    return lax.broadcasted_iota(I32, shape, axis)


def ones_where(condition):
    return jnp.where(condition, 1.0, 0.0).astype(BF16)


def matmul(left, right):
    return jnp.dot(left, right, preferred_element_type=F32)


def matmul_nt(left, right):
    return lax.dot_general(left, right, (((1,), (1,)), ((), ())), preferred_element_type=F32)


def in_vmem(array):
    return pltpu.with_memory_space_constraint(array, pltpu.VMEM)


def in_hbm(array):
    return pltpu.with_memory_space_constraint(array, pltpu.HBM)


def start_copies(pairs, sems):
    copies = [
        pltpu.make_async_copy(source, target, sems.at[n])
        for n, (source, target) in enumerate(pairs)
    ]
    for copy in copies:
        copy.start()
    return copies


def round_up(value, multiple):
    return -(-value // multiple) * multiple


def whole(*spaces):
    return [pl.BlockSpec(memory_space=space) for space in spaces]


def block_sizes(width, capacity):
    slots = round_up(capacity, TILE // FOLD)
    group_rows = FOLD * slots
    groups = width // FOLD // LANES
    return slots, group_rows, groups, groups * group_rows + TILE


def pack_all(
    frames, route_peer, route_pos, destination, key_cache, value_cache, conv_state, peers, capacity
):
    row_count, model = frames.shape
    slots, group_rows, groups, block_rows = block_sizes(model, capacity)
    half = model // FOLD
    streams, left, width = key_cache.shape
    tail = conv_state.shape[0] // streams
    rows = 2 * left + tail + 1

    def body(
        dest_hbm, own_hbm, peer_hbm, pos_hbm, key_hbm, value_hbm, conv_hbm, frames_hbm,
        packed_hbm, up_ref, down_ref, packed_ref, conv_ref, frames_ref, conv_f32, dest_ref, own_ref,
        peer_ref, pos_ref, sems, small_sems, move_sems,
    ):
        frames_copy = pltpu.make_async_copy(frames_hbm, frames_ref, sems.at[0])
        conv_copy = pltpu.make_async_copy(conv_hbm, conv_ref, sems.at[1])
        small_copies = start_copies(
            ((peer_hbm, peer_ref), (pos_hbm, pos_ref), (dest_hbm, dest_ref), (own_hbm, own_ref)),
            small_sems,
        )
        frames_copy.start()
        conv_copy.start()
        for copy in small_copies:
            copy.wait()
        own = own_ref[0]
        moves = []
        for n, (out_ref, device) in enumerate(
            ((up_ref, (own + 1) % peers), (down_ref, (own + peers - 1) % peers))
        ):
            rank = jnp.int32(0)
            for j in range(streams):
                target = dest_ref[j]
                chosen = target // streams == device
                place = jnp.minimum(rank, MIG - 1)
                copies = [
                    pltpu.make_async_copy(
                        source.at[j],
                        out_ref.at[place, k * left : (k + 1) * left, :],
                        move_sems.at[n, k, j],
                    )
                    for k, source in enumerate((key_hbm, value_hbm))
                ]

                @pl.when(chosen)
                def _():
                    for copy in copies:
                        copy.start()

                moves.append((out_ref, chosen, place, j, target % streams, copies))
                rank = rank + chosen.astype(I32)

        peer = peer_ref[...]
        owner = ones_where(iota((peers, row_count), 0) == peer)
        earlier = ones_where(iota((row_count, row_count), 0) < iota((row_count, row_count), 1))
        running = matmul(owner, earlier)
        slot = jnp.sum(running * owner.astype(F32), axis=0, keepdims=True).astype(I32)
        flat = peer * group_rows + slot
        packed_row = iota((peers * group_rows, row_count), 0)
        pick = jnp.concatenate(
            [ones_where(packed_row == flat + h * slots) for h in range(FOLD)], axis=1
        )
        owner_tile = ones_where(iota((peers * TILE, row_count), 0) // TILE == peer)
        lane = iota((LANES, row_count), 0)
        in_lane = (lane % slots == slot) & (lane < group_rows)
        code = jnp.where(in_lane, (pos_ref[...] + 1).astype(F32), 0.0).astype(BF16)
        codes = matmul_nt(owner_tile, code).astype(BF16)
        frames_copy.wait()
        source = jnp.concatenate(
            [frames_ref[:, h * half : (h + 1) * half] for h in range(FOLD)], axis=0
        )
        packed = matmul(pick, source).astype(BF16)
        for p in range(peers):
            for g in range(groups):
                first = p * block_rows + g * group_rows
                packed_ref[first : first + group_rows, :] = packed[
                    p * group_rows : (p + 1) * group_rows, g * LANES : (g + 1) * LANES
                ]
            packed_ref[(p + 1) * block_rows - TILE : (p + 1) * block_rows, :] = codes[
                p * TILE : (p + 1) * TILE, :
            ]
        packed_copy = pltpu.make_async_copy(packed_ref, packed_hbm, sems.at[2])
        packed_copy.start()
        conv_copy.wait()
        stream_of = iota((streams, LANES), 0)
        slot_row = jnp.zeros((streams, LANES), I32)
        for j in range(streams):
            slot_row = jnp.where(stream_of == j, dest_ref[j] % streams + 1, slot_row)
        for c in range(width // LANES):
            conv_f32[c, 0 : tail * streams, :] = conv_ref[:, c * LANES : (c + 1) * LANES].astype(F32)
            conv_f32[c, tail * streams : (tail + 1) * streams, :] = slot_row.astype(F32)
        for out_ref in (up_ref, down_ref):
            out_ref[:, 2 * left : rows, :] = jnp.zeros((MIG, 1 + tail, width), BF16)
        for out_ref, chosen, place, j, slot, copies in moves:

            @pl.when(chosen)
            def _():
                for c in range(width // LANES):
                    out_ref[place, 2 * left : rows, c * LANES : (c + 1) * LANES] = conv_f32[
                        c, pl.ds(j, tail + 1, stride=streams), :
                    ].astype(BF16)
                for copy in copies:
                    copy.wait()

        packed_copy.wait()

    packed_shape = (peers * block_rows, LANES)
    bundle = pltpu.VMEM((MIG, rows, width), BF16)
    return pl.pallas_call(
        body,
        out_shape=(pltpu.HBM(packed_shape, BF16), bundle, bundle),
        in_specs=whole(*[pl.ANY] * 8),
        out_specs=whole(pl.ANY, pltpu.VMEM, pltpu.VMEM),
        scratch_shapes=[
            pltpu.VMEM(packed_shape, BF16),
            pltpu.VMEM(conv_state.shape, BF16),
            pltpu.VMEM(frames.shape, BF16),
            pltpu.VMEM((width // LANES, (tail + 1) * streams, LANES), F32),
            pltpu.SMEM((streams,), I32),
            pltpu.SMEM((1,), I32),
            pltpu.VMEM((1, row_count), I32),
            pltpu.VMEM((1, row_count), I32),
            pltpu.SemaphoreType.DMA((3,)),
            pltpu.SemaphoreType.DMA((4,)),
            pltpu.SemaphoreType.DMA((2, 2, streams)),
        ],
        compiler_params=pltpu.CompilerParams(vmem_limit_bytes=12 << 20),
        name="pack_all",
    )(
        *map(
            in_hbm,
            (
                destination, own_index(), route_peer.reshape(1, -1), route_pos.reshape(1, -1),
                key_cache, value_cache, conv_state, frames,
            ),
        )
    )


def own_index():
    return lax.axis_index("streams").astype(I32).reshape(1)


def valid_tile(valid_ref, streams, lanes):
    stream_of = iota((streams, lanes), 0)
    valid = jnp.zeros((streams, lanes), I32)
    for s in range(streams):
        valid = jnp.where(stream_of == s, valid_ref[s], valid)
    return valid


def settle_streams(
    from_lower, from_upper, destination, valid_count, key_cache, value_cache, conv_state,
    conv_kernel, qkv_weight, span,
):
    streams, left, width = key_cache.shape
    block = from_lower.shape[1]
    tail = conv_state.shape[0] // streams
    taps = conv_kernel.shape[0]
    groups = width // LANES
    cache = (streams, left, width)
    stored = tail + 1

    def body(
        dest_hbm, own_hbm, valid_hbm, lower_ref, upper_ref, key_hbm, value_hbm, conv_hbm, taps_hbm,
        weight_hbm, keys_old, values_old, conv_kept, conv_part, taps_f32, first_weight, second_weight,
        key_ref, value_ref, conv_ref, taps_ref, conv_f32, conv_old, dest_ref, own_ref, valid_ref,
        sems, small_sems, weight_sems,
    ):
        small_copies = start_copies(
            ((dest_hbm, dest_ref), (own_hbm, own_ref), (valid_hbm, valid_ref)), small_sems
        )
        copies = start_copies(
            (
                (conv_hbm, conv_ref), (key_hbm, key_ref), (value_hbm, value_ref),
                (taps_hbm, taps_ref),
            ),
            sems,
        )
        codes = [
            (bundle_ref, j, jnp.max(bundle_ref[j, 2 * left + tail :, :].astype(F32)).astype(I32))
            for bundle_ref in (lower_ref, upper_ref)
            for j in range(MIG)
        ]
        for copy in small_copies:
            copy.wait()
        own = own_ref[0]
        valid = valid_tile(valid_ref, streams, streams * stored)
        column = iota((streams, streams * stored), 1)
        first = iota((streams, streams * stored), 0) * stored + valid
        kept_pick = jnp.concatenate(
            [ones_where((column == first + i) & (valid + i < tail)) for i in range(tail)], axis=0
        )
        for bundle_ref, j, code in codes:

            @pl.when(code > 0)
            def _():
                slot = code - 1
                keys_old[slot] = bundle_ref[j, 0:left, :]
                values_old[slot] = bundle_ref[j, left : 2 * left, :]
                for c in range(groups):
                    conv_old[c, pl.ds(pl.multiple_of(slot * stored, TILE), stored), :] = bundle_ref[
                        j, 2 * left : 2 * left + stored, c * LANES : (c + 1) * LANES
                    ].astype(F32)

        weight_copies = start_copies(
            [
                (weight_hbm.at[(n * MIG + j) * block : (n * MIG + j + 1) * block, 0:width], target.at[j])
                for n, target in enumerate((first_weight, second_weight))
                for j in range(MIG)
            ],
            weight_sems,
        )
        for copy in copies:
            copy.wait()
        for c in range(groups):
            lanes = slice(c * LANES, (c + 1) * LANES)
            taps_f32[c] = taps_ref[:, lanes].astype(F32)
            conv_f32[c, 0 : tail * streams, :] = conv_ref[:, lanes].astype(F32)
            conv_f32[c, tail * streams : stored * streams, :] = jnp.zeros((streams, LANES), F32)
        for j in range(streams):
            target = dest_ref[j]

            @pl.when(target // streams == own)
            def _():
                slot = target % streams
                keys_old[slot] = key_ref[j]
                values_old[slot] = value_ref[j]
                for c in range(groups):
                    conv_old[c, pl.ds(pl.multiple_of(slot * stored, TILE), stored), :] = conv_f32[
                        c, pl.ds(j, stored, stride=streams), :
                    ]

        for c in range(groups):
            lanes = slice(c * LANES, (c + 1) * LANES)
            conv_kept[:, lanes] = matmul(kept_pick, conv_old[c].astype(BF16)).astype(BF16)
            inputs = [conv_old[c, pl.ds(j, streams, stride=stored), :] for j in range(tail)]
            totals = [jnp.zeros((streams, LANES), F32)] * span
            for i in range(taps):
                tap = taps_f32[c, pl.ds(i, streams, stride=0), :]
                for t in range(min(span, tail - i)):
                    totals[t] = totals[t] + tap * inputs[t + i]
            for t in range(span):
                conv_part[c, t * streams : (t + 1) * streams, :] = totals[t]
        for copy in weight_copies:
            copy.wait()

    return pl.pallas_call(
        body,
        out_shape=(
            pltpu.VMEM(cache, BF16),
            pltpu.VMEM(cache, BF16),
            pltpu.VMEM((tail * streams, width), BF16),
            pltpu.VMEM((groups, span * streams, LANES), F32),
            pltpu.VMEM((groups, taps, LANES), F32),
            pltpu.VMEM(from_lower.shape, BF16),
            pltpu.VMEM(from_lower.shape, BF16),
        ),
        in_specs=whole(*[pl.ANY] * 3, *[pltpu.VMEM] * 2, *[pl.ANY] * 5),
        out_specs=whole(*[pltpu.VMEM] * 7),
        input_output_aliases={3: 5, 4: 6},
        scratch_shapes=[
            pltpu.VMEM(cache, BF16),
            pltpu.VMEM(cache, BF16),
            pltpu.VMEM(conv_state.shape, BF16),
            pltpu.VMEM(conv_kernel.shape, BF16),
            pltpu.VMEM((groups, stored * streams, LANES), F32),
            pltpu.VMEM((groups, stored * streams, LANES), F32),
            pltpu.SMEM((streams,), I32),
            pltpu.SMEM((1,), I32),
            pltpu.SMEM((streams,), I32),
            pltpu.SemaphoreType.DMA((4,)),
            pltpu.SemaphoreType.DMA((3,)),
            pltpu.SemaphoreType.DMA((2 * MIG,)),
        ],
        compiler_params=pltpu.CompilerParams(vmem_limit_bytes=16 << 20),
        name="settle_streams",
    )(
        *map(in_hbm, (destination, own_index(), valid_count)),
        in_vmem(from_lower), in_vmem(from_upper),
        *map(in_hbm, (key_cache, value_cache, conv_state, conv_kernel, qkv_weight)),
    )


def stream_step(received, valid_count, settled, qkv_weight, peers, row_count, capacity):
    keys_settled, _, conv_settled, _, taps_settled, near_weight, _ = settled
    near = near_weight.shape[0] * near_weight.shape[1]
    streams, left, width = keys_settled.shape
    tail = conv_settled.shape[0] // streams
    taps = taps_settled.shape[1]
    span = row_count // streams
    model, columns = qkv_weight.shape
    half = model // FOLD
    heads = width // HEAD
    keys = left + span
    lane_groups = width // LANES
    edges = [columns * n // SPLIT for n in CHUNK_EDGES]
    slots, group_rows, groups, block_rows = block_sizes(model, capacity)
    packed_rows = peers * group_rows

    def body(
        valid_hbm, recv_ref, keys_old, values_old, conv_kept, conv_part, taps_f32, first_weight,
        second_weight, weight_hbm,
        encoded_hbm, keys_next_hbm, values_next_hbm, conv_next_hbm,
        encoded_ref, keys_next_ref, values_next_ref, conv_next_ref,
        weight_ref, gathered, qkv_ref, attended_ref, attended_f32, encoded_f32, valid_ref,
        weight_sems, out_sems, valid_sem,
    ):
        parts = [(2 * near if n == 0 else 0, a, b) for n, (a, b) in enumerate(zip(edges, edges[1:]))]
        weight_copies = [
            pltpu.make_async_copy(
                weight_hbm.at[top:, first:last], weight_ref.at[top:, first:last], weight_sems.at[n]
            )
            for n, (top, first, last) in enumerate(parts)
        ]
        for copy in weight_copies:
            copy.start()
        valid_copy = pltpu.make_async_copy(valid_hbm, valid_ref, valid_sem)
        valid_copy.start()

        for p in range(peers):
            for g in range(groups):
                gathered[p * group_rows : (p + 1) * group_rows, g * LANES : (g + 1) * LANES] = recv_ref[
                    p * block_rows + g * group_rows : p * block_rows + (g + 1) * group_rows, :
                ]
        codes = jnp.concatenate(
            [recv_ref[(p + 1) * block_rows - TILE : (p + 1) * block_rows, :] for p in range(peers)],
            axis=0,
        )
        spread_lane = ones_where(
            iota((LANES, packed_rows), 1) % group_rows == iota((LANES, packed_rows), 0)
        )
        spread = matmul(codes, spread_lane)
        column = iota((peers * TILE, packed_rows), 1)
        own_tile = iota((peers * TILE, packed_rows), 0) == column // group_rows * TILE
        position = jnp.sum(jnp.where(own_tile, spread, 0.0), axis=0, keepdims=True).astype(I32)
        out_row = iota((row_count, packed_rows), 0) + 1
        column_half = iota((row_count, packed_rows), 1) % group_rows // slots
        hit = out_row == position
        place = jnp.concatenate([ones_where(hit & (column_half == h)) for h in range(FOLD)], axis=0)
        halves = matmul(place, gathered[...])
        owned = jnp.concatenate(
            [halves[h * row_count : (h + 1) * row_count, :] for h in range(FOLD)], axis=1
        )
        centered = owned - jnp.mean(owned, axis=-1, keepdims=True)
        spread_of = jnp.mean(centered * centered, axis=-1, keepdims=True)
        normed = (centered * lax.rsqrt(spread_of + EPSILON)).astype(BF16)

        def project(n):
            top, first, last = parts[n]
            weight_copies[n].wait()
            weight = weight_ref[top:, first:last]
            if top:
                near_weights = [ref[...].reshape(near, width) for ref in (first_weight, second_weight)]
                weight = jnp.concatenate([*near_weights, weight], axis=0)
            qkv_ref[:, first:last] = matmul(normed, weight).astype(BF16)

        for n in range(VALUES_FROM):
            project(n)
        valid_copy.wait()

        head_rows = heads * span
        head_mask = ones_where(
            iota((head_rows, width), 1) // HEAD == iota((head_rows, width), 0) // span
        )
        t_of = iota((keys, head_rows), 1) % span
        key_of = iota((keys, head_rows), 0) - left
        causal = key_of <= t_of
        t_row = iota((span, LANES), 0)
        lane = iota((span, LANES), 1)
        all_rows = [slice(s * span, (s + 1) * span) for s in range(streams)]
        all_keys = [
            jnp.concatenate([keys_old[s], qkv_ref[all_rows[s], width : 2 * width]], axis=0)
            for s in range(streams)
        ]
        all_scores = []
        for first in range(0, streams, 2):
            pair = range(first, first + 2)
            queries = [
                jnp.concatenate([qkv_ref[all_rows[s], 0:width]] * heads, axis=0) * head_mask
                for s in pair
            ]
            scores = matmul_nt(
                jnp.concatenate([all_keys[s] for s in pair], axis=0),
                jnp.concatenate(queries, axis=0),
            )
            all_scores += [
                scores[n * keys : (n + 1) * keys, n * head_rows : (n + 1) * head_rows]
                for n in range(2)
            ]
        all_probabilities = []
        for s in range(streams):
            allowed = (key_of < 0) | (causal & (key_of < valid_ref[s]))
            scores = jnp.where(allowed, all_scores[s] * HEAD ** (-0.5), -1e30)
            weights = jnp.exp(scores - jnp.max(scores, axis=0, keepdims=True))
            all_probabilities.append(
                (weights / jnp.sum(weights, axis=0, keepdims=True)).astype(BF16)
            )
        shift = iota((left, GROUP * keys), 1) - iota((left, GROUP * keys), 0)
        groups_of = [range(first, first + GROUP) for first in range(0, streams, GROUP)]
        picks = [
            jnp.concatenate(
                [ones_where(shift == valid_ref[s] + n * keys) for n, s in enumerate(group)], axis=0
            )
            for group in groups_of
        ]

        def shifted(source, target):
            for group, pick in zip(groups_of, picks):
                target[group[0] * left : (group[-1] + 1) * left, :] = matmul(
                    pick, jnp.concatenate([source[s] for s in group], axis=0)
                ).astype(BF16)

        shifted(all_keys, keys_next_ref)
        keys_copy = pltpu.make_async_copy(keys_next_ref, keys_next_hbm, out_sems.at[0])
        keys_copy.start()
        out_copies = [keys_copy]
        valid = valid_tile(valid_ref, streams, row_count)
        column = iota((streams, row_count), 1)
        frame = valid - tail
        first = iota((streams, row_count), 0) * span + frame
        new_pick = jnp.concatenate(
            [ones_where((column == first + i) & (frame + i >= 0)) for i in range(tail)], axis=0
        )
        valid = valid_tile(valid_ref, streams, LANES)

        for piece in range(lane_groups // PIECE):
            project(VALUES_FROM + piece)
            lanes = slice(piece * PIECE * LANES, (piece + 1) * PIECE * LANES)
            all_values = [
                jnp.concatenate(
                    [
                        values_old[s, :, lanes],
                        qkv_ref[all_rows[s], 2 * width + lanes.start : 2 * width + lanes.stop],
                    ],
                    axis=0,
                )
                for s in range(streams)
            ]
            all_mixed = [
                lax.dot_general(
                    all_probabilities[s], all_values[s], (((0,), (0,)), ((), ())),
                    preferred_element_type=F32,
                )
                for s in range(streams)
            ]
            for group, pick in zip(groups_of, picks):
                values_next_ref[group[0] * left : (group[-1] + 1) * left, lanes] = matmul(
                    pick, jnp.concatenate([all_values[s] for s in group], axis=0)
                ).astype(BF16)
            for s in range(streams):
                for n in range(PIECE):
                    c = piece * PIECE + n
                    here = slice(n * LANES, (n + 1) * LANES)
                    first = c * LANES // HEAD
                    last = ((c + 1) * LANES - 1) // HEAD
                    attended = all_mixed[s][first * span : (first + 1) * span, here]
                    for h in range(first + 1, last + 1):
                        attended = jnp.where(
                            lane >= h * HEAD - c * LANES,
                            all_mixed[s][h * span : (h + 1) * span, here],
                            attended,
                        )
                    attended = jnp.where(t_row < valid_ref[s], attended, 0.0).astype(BF16)
                    attended_ref[all_rows[s], c * LANES : (c + 1) * LANES] = attended
                    attended_f32[c, all_rows[s], :] = attended.astype(F32)
            conv_next_ref[:, lanes] = conv_kept[:, lanes] + matmul(
                new_pick, attended_ref[:, lanes]
            ).astype(BF16)
            for c in range(piece * PIECE, (piece + 1) * PIECE):
                inputs = [attended_f32[c, pl.ds(t, streams, stride=span), :] for t in range(span)]
                totals = [
                    conv_part[c, t * streams : (t + 1) * streams, :] + inputs[t]
                    for t in range(span)
                ]
                for i in range(max(tail - span + 1, 0), taps):
                    tap = taps_f32[c, pl.ds(i, streams, stride=0), :]
                    for t in range(max(tail - i, 0), min(span, span + tail - i)):
                        totals[t] = totals[t] + tap * inputs[t + i - tail]
                for t in range(span):
                    encoded_f32[c, pl.ds(t, streams, stride=span), :] = jnp.where(
                        t < valid, totals[t], 0.0
                    )
                encoded_ref[:, c * LANES : (c + 1) * LANES] = encoded_f32[c].astype(BF16)
            for n, (source, target) in enumerate(
                (
                    (values_next_ref, values_next_hbm), (conv_next_ref, conv_next_hbm),
                    (encoded_ref, encoded_hbm),
                )
            ):
                copy = pltpu.make_async_copy(
                    source.at[:, lanes], target.at[:, lanes], out_sems.at[1 + 3 * piece + n]
                )
                copy.start()
                out_copies.append(copy)
        for copy in out_copies:
            copy.wait()

    cache = (streams * left, width)
    by_lane_group = pltpu.VMEM((lane_groups, row_count, LANES), F32)
    out_shapes = ((row_count, width), cache, cache, (tail * streams, width))
    return pl.pallas_call(
        body,
        out_shape=[jax.ShapeDtypeStruct(shape, BF16) for shape in out_shapes],
        in_specs=whole(pl.ANY, *[pltpu.VMEM] * 8, pl.ANY),
        out_specs=whole(*[pl.ANY] * 4),
        scratch_shapes=[
            *[pltpu.VMEM(shape, BF16) for shape in out_shapes],
            pltpu.VMEM((model, columns), BF16),
            pltpu.VMEM((packed_rows, half), BF16),
            pltpu.VMEM((row_count, columns), BF16),
            pltpu.VMEM((row_count, width), BF16),
            by_lane_group,
            by_lane_group,
            pltpu.SMEM((streams,), I32),
            pltpu.SemaphoreType.DMA((len(edges) - 1,)),
            pltpu.SemaphoreType.DMA((1 + 3 * (lane_groups // PIECE),)),
            pltpu.SemaphoreType.DMA,
        ],
        compiler_params=pltpu.CompilerParams(vmem_limit_bytes=32 << 20),
        name="stream_step",
    )(
        in_hbm(valid_count), in_vmem(received), *map(in_vmem, settled), in_hbm(qkv_weight)
    )


def from_behind(block, axis, distance):
    count = lax.axis_size(axis)
    return lax.ppermute(block, axis, [((i - distance) % count, i) for i in range(count)])


def local(
    frames, route_peer, route_pos, destination, valid_count, key_cache, value_cache, conv_state,
    qkv_weight, conv_kernel,
):
    peers = lax.axis_size("streams")
    row_count = frames.shape[0]
    per_peer = row_count // peers
    capacity = per_peer + per_peer // 2
    streams, left, width = key_cache.shape
    conv_by_time = conv_state.transpose(1, 0, 2).reshape(-1, width)
    packed, up, down = pack_all(
        frames, route_peer, route_pos, destination, key_cache, value_cache, conv_by_time,
        peers, capacity,
    )
    from_lower = from_behind(up, "streams", 1)
    from_upper = from_behind(down, "streams", -1)
    received = lax.all_to_all(packed, "streams", split_axis=0, concat_axis=0, tiled=True)
    settled = settle_streams(
        from_lower, from_upper, destination, valid_count, key_cache, value_cache,
        conv_by_time, conv_kernel, qkv_weight, row_count // streams,
    )
    encoded, keys_next, values_next, conv_next = stream_step(
        received, valid_count, settled, qkv_weight, peers, row_count, capacity
    )
    cache = (streams, left, width)
    return (
        encoded, keys_next.reshape(cache), values_next.reshape(cache),
        conv_next.reshape(-1, streams, width).transpose(1, 0, 2),
    )


def solution(mesh):
    rows = P(("groups", "streams"))
    return jax.shard_map(
        local,
        mesh=mesh,
        in_specs=(rows,) * 8 + (P(), P()),
        out_specs=(rows,) * 4,
        check_vma=False,
    )
```
